768 devices in a mesh: row: 64 (over x, y, core), col: 12 (over z).
Axes of the slice: x: 4, y: 8, z: 12, core: 2. Of those that a mesh axis runs over, the one named last changes fastest.
Arguments:
- matrix: float32 [12, 64, 16, 12288], P(None, 'row', None, 'col'), may hold values from -6 to 6
- panel: float32 [12, 64, 16, 384], P(None, 'row'), may hold values from -500 to 500
Outputs:
- updated: float32 [12, 64, 16, 12288], P(None, 'row', None, 'col')
The draws below stay inside these ranges and needn't reach their ends.
All inputs are finite; a program needn't handle non-finite values.
Results may differ from the reference program's by a relative error of at most 0.00005.
Values sent between devices are 32-bit elements; how exact they have to be, the bound alone decides.
A program may use at most 64 MiB of HBM per device.

```python
import jax
import jax.numpy as jnp
from jax import lax

ORDER = 12288
PANEL = 384
TILE = 16
ROUNDS = 12
N_ROW = 64


def draw_panel(key, part):
    base_key, row_key, col_key = jax.random.split(key, 3)
    full_shape = (ROUNDS, N_ROW, TILE, PANEL)
    row_shape = (ROUNDS, N_ROW, TILE, 1)
    values = jnp.clip(jax.random.normal(base_key, full_shape, jnp.float32), -5.0, 5.0)
    row_scale = jnp.exp(jax.random.uniform(row_key, row_shape, jnp.float32, 0.0, 2.3))
    col_scale = jnp.exp(jax.random.uniform(col_key, (1, 1, 1, PANEL), jnp.float32, 0.0, 2.3))
    return values * row_scale * col_scale


def shard_levels(stream_key, dims, pieces, smallest, high):
    factor_of, own = 1.0, jax.random.fold_in(stream_key, 6)
    for position, shards_of in pieces:
        heights = jnp.exp(jax.random.uniform(jax.random.fold_in(own, position), (shards_of,), jnp.float32, smallest / len(pieces), high / len(pieces)))
        factor_of = factor_of * jnp.repeat(heights, dims[position] // shards_of).reshape([-1 if axis == position else 1 for axis in range(len(dims))])
    return factor_of


def bell_draw(own_key, shape, spread, reach, shards=(), held_as=jnp.bfloat16):
    array = jax.random.normal(own_key, shape, jnp.float32) * spread
    if len(shards) > 0:
        array = shard_levels(own_key, shape, shards, -0.22, 0.18) * array
    return jnp.clip(array, min=-reach, max=reach).astype(held_as)


def setup_inputs(seed: int = 0) -> dict:
    keys = jax.random.split(jax.random.key(seed), 3)
    matrix = bell_draw(keys[0], (ROUNDS, N_ROW, TILE, ORDER), 1.0, 6.0, ((1, 64), (3, 12)), jnp.float32)
    panel = draw_panel(jax.random.fold_in(keys[2], 71), 0)
    return dict(matrix=matrix, panel=panel)


def exact_dot(left, right):
    return jnp.dot(left, right, precision=lax.Precision.HIGHEST)

def reference(matrix, panel):
    full = matrix.reshape(ORDER, ORDER)
    tall = panel.reshape(ORDER, PANEL)
    gram = exact_dot(tall.T, tall)
    lower_factor = jnp.linalg.cholesky(gram)
    identity_matrix = jnp.eye(PANEL, dtype=gram.dtype)
    inverse_factor = lax.linalg.triangular_solve(lower_factor, identity_matrix, left_side=True, lower=True)
    basis = exact_dot(tall, inverse_factor.T)
    row_ids = jnp.arange(ORDER, dtype=jnp.int32)[:, None]
    col_ids = jnp.arange(ORDER, dtype=jnp.int32)[None, :]
    half_lower = jnp.where(row_ids > col_ids, full, jnp.where(row_ids == col_ids, 0.5 * full, 0.0 * full))
    image = exact_dot(half_lower, basis) + exact_dot(half_lower.T, basis)
    curvature = exact_dot(basis.T, image)
    residual_image = image - exact_dot(basis, curvature)
    changed = full - 2.0 * (exact_dot(basis, residual_image.T) + exact_dot(residual_image, basis.T))
    result = jnp.where(row_ids >= col_ids, changed, 0.0 * changed)
    return result.reshape(matrix.shape)
```

```python
import functools

import jax
import jax.numpy as jnp
from jax import lax
from jax.experimental import pallas as pl
from jax.experimental.pallas import tpu as pltpu
from jax.sharding import PartitionSpec as P

EXACT = lax.Precision.HIGHEST
PLANES = {64: (4, 8), 8: (2, 2)}


def dot_nn(a, b):
    return lax.dot_general(a, b, (((1,), (0,)), ((), ())), precision=EXACT,
                           preferred_element_type=jnp.float32)


def dot_tn(a, b):
    return lax.dot_general(a, b, (((0,), (0,)), ((), ())), precision=EXACT,
                           preferred_element_type=jnp.float32)


def dot_nt(a, b):
    return lax.dot_general(a, b, (((1,), (1,)), ((), ())), precision=EXACT,
                           preferred_element_type=jnp.float32)


def by_distance(n):
    return sorted(range(1, n), key=lambda d: (min(d, n - d), d))


def comm_kernel(sizes, mat_ref, pan_ref, g_ref, k_ref, tc_ref, wc_ref, wr_ref,
                h_ref, gl_ref, gc_ref, gsum_ref, gx_ref, gsx_ref, gy_ref, gf_ref,
                mp_ref, cx_ref, mx_ref, ms_ref, my_ref,
                dp_ref, rz_ref, kp_ref, kc_ref, kx_ref, ks_ref, ky_ref, kz_ref, kf_ref,
                send_sems, t_sems, w_sems, wz_sems, mc_sems, mx_sems, my_sems, dz_sems,
                g_sems, gz_sems, k_sems, kz_sems, ka_sems):
    NX, NY, NZ, TR, WIDTH, PW = sizes
    row = lax.axis_index("row")
    z = lax.axis_index("col")
    core = lax.rem(row, 2)
    chip = lax.div(row, 2)
    y = lax.rem(chip, NY)
    x = lax.div(chip, NY)
    other = 1 - core

    def at(x_, y_, c_):
        return (x_ * NY + y_) * 2 + c_

    def xp(d):
        return lax.rem(x + d, NX)

    def yp(d):
        return lax.rem(y + d, NY)

    def zp(d):
        return lax.rem(z + d, NZ)

    to_x = lambda d: (at(xp(d), y, core), z)
    to_y = lambda d: (at(x, yp(d), core), z)
    to_z = lambda d: (row, zp(d))
    to_core = (at(x, y, other), z)

    barrier = pltpu.get_barrier_semaphore()
    peers = ([to_x(d) for d in range(1, NX)] + [to_y(d) for d in range(1, NY)]
             + [to_z(d) for d in range(1, NZ)] + [to_core])
    for peer in peers:
        pl.semaphore_signal(barrier, inc=1, device_id=peer, device_id_type=pl.DeviceIdType.MESH)
    pl.semaphore_wait(barrier, len(peers))

    sent = []

    def send(src, dst, sem, peer, when=None):
        slot = len(sent)
        sent.append((src, when))
        pltpu.make_async_remote_copy(
            src_ref=src, dst_ref=dst, send_sem=send_sems.at[slot], recv_sem=sem,
            device_id=peer, device_id_type=pl.DeviceIdType.MESH).start()

    def left(slot, src):
        pltpu.make_async_remote_copy(
            src_ref=src, dst_ref=src, send_sem=send_sems.at[slot], recv_sem=t_sems.at[0],
            device_id=to_core, device_id_type=pl.DeviceIdType.MESH).wait_send()

    def arrive(dst, sem):
        pltpu.make_async_remote_copy(
            src_ref=dst, dst_ref=dst, send_sem=send_sems.at[0], recv_sem=sem,
            device_id=to_core, device_id_type=pl.DeviceIdType.MESH).wait_recv()

    YD, XD, ZD = by_distance(NY), by_distance(NX), by_distance(NZ)

    own_t = pan_ref.at[z]
    for d in YD:
        send(own_t, tc_ref.at[x, y, core], t_sems.at[row], to_y(d))
    for d in XD:
        send(own_t, tc_ref.at[x, y, core], t_sems.at[row], to_x(d))
    tc_ref[x, y, core] = pan_ref[z]

    t_rows = pan_ref[...].reshape(NZ * TR, PW)
    gl_ref[...] = dot_tn(t_rows, t_rows).reshape(NZ, 2, PW // NZ // 2, PW)
    send(gl_ref.at[z, other], gc_ref, g_sems.at[0], to_core)

    sub = lax.broadcasted_iota(jnp.int32, (TR, WIDTH), 0) + row * TR
    lane = lax.broadcasted_iota(jnp.int32, (TR, WIDTH), 1)
    weight_diag = jnp.where(sub > lane, 1.0, jnp.where(sub == lane, 0.5, 0.0))
    for a in range(NZ):
        tile = mat_ref[a]
        diag_part = jnp.where(weight_diag > 0.0, tile * weight_diag, 0.0)
        h_ref[a] = jnp.where(z < a, tile, jnp.where(z == a, diag_part, 0.0))

    XW = WIDTH // NX
    for d in list(XD) + [0]:
        xb = xp(d)
        cols = pl.ds(pl.multiple_of(xb * XW, XW), XW)
        h = h_ref[:, :, cols].reshape(NZ * TR, XW)
        mp_ref[xb] = dot_tn(h, t_rows).reshape(NY, 2, TR, PW)
        send(mp_ref.at[xb, :, other], cx_ref.at[xb], mc_sems.at[xb], to_core)

    arrive(gc_ref, g_sems.at[0])
    gsum_ref[...] = gl_ref[z, core] + gc_ref[...]
    for d in XD:
        send(gsum_ref, gx_ref.at[d - 1], g_sems.at[d], to_x(d))

    for d in list(XD) + [0]:
        xb = xp(d)
        arrive(cx_ref.at[xb], mc_sems.at[xb])
        ms_ref[xb] = mp_ref[xb, :, core] + cx_ref[xb]
        if d:
            send(ms_ref.at[xb], mx_ref.at[d - 1], mx_sems.at[d - 1], to_x(d))

    for d in YD:
        tile = tc_ref.at[x, yp(NY - d), core]
        sem = t_sems.at[at(x, yp(NY - d), core)]
        arrive(tile, sem)
        for dx in XD:
            send(tile, tile, sem, to_x(dx))

    TS = NX * NY * 2

    send(tc_ref.at[x, :, core], tc_ref.at[x, :, core], t_sems.at[TS + x], to_core)

    gs = gsum_ref[...]
    for d in XD:
        arrive(gx_ref.at[d - 1], g_sems.at[d])
        gs = gs + gx_ref[d - 1]
    gsx_ref[...] = gs
    for d in YD:
        send(gsx_ref, gy_ref.at[d - 1], g_sems.at[NX + d], to_y(d))

    for dx in XD:
        xb = xp(NX - dx)
        for dy in [0] + YD:
            arrive(tc_ref.at[xb, yp(NY - dy), core], t_sems.at[at(xb, yp(NY - dy), core)])
        send(tc_ref.at[xb, :, core], tc_ref.at[xb, :, core], t_sems.at[TS + xb], to_core)

    for d in XD:
        arrive(mx_ref.at[d - 1], mx_sems.at[d - 1])
    msum = ms_ref[x]
    for d in XD:
        msum = msum + mx_ref[d - 1]
    mp_ref[x, :, core] = msum
    for d in YD:
        send(mp_ref.at[x, yp(d), core], my_ref.at[d - 1], my_sems.at[d - 1], to_y(d))

    for dx in [0] + XD:
        xb = xp(NX - dx)
        arrive(tc_ref.at[xb, :, other], t_sems.at[TS + xb])

    direct = dot_nn(h_ref[...].reshape(NZ * TR, WIDTH), tc_ref[...].reshape(WIDTH, PW))
    dp_ref[...] = direct.reshape(NZ, TR, PW)
    for d in ZD:
        send(dp_ref.at[zp(d)], rz_ref.at[d - 1], dz_sems.at[d - 1], to_z(d))
    NP = PW // 2 // NX // 8
    kp_ref[...] = dot_tn(t_rows, direct).reshape(2, NX, NP, 8, PW)
    send(kp_ref.at[other], kc_ref, k_sems.at[0], to_core)

    gs = gsx_ref[...]
    for d in YD:
        arrive(gy_ref.at[d - 1], g_sems.at[NX + d])
        gs = gs + gy_ref[d - 1]
    gf_ref[...] = gs
    g_ref[z, core] = gs
    for d in ZD:
        send(gf_ref, g_ref.at[z, core], gz_sems.at[d - 1], to_z(d))

    msum = mp_ref[x, y, core]
    for d in YD:
        arrive(my_ref.at[d - 1], my_sems.at[d - 1])
        msum = msum + my_ref[d - 1]

    arrive(kc_ref, k_sems.at[0])
    ks_ref[...] = kp_ref[core] + kc_ref[...]
    for d in XD:
        send(ks_ref.at[xp(d)], kx_ref.at[d - 1], k_sems.at[d], to_x(d))

    wsum = msum + dp_ref[z]
    for d in ZD:
        arrive(rz_ref.at[d - 1], dz_sems.at[d - 1])
        wsum = wsum + rz_ref[d - 1]
    wc_ref[x, y, core] = wsum
    wr_ref[z] = wsum
    for d in YD:
        send(wc_ref.at[x, y, core], wc_ref.at[x, y, core], w_sems.at[row], to_y(d))
    for d in XD:
        send(wc_ref.at[x, y, core], wc_ref.at[x, y, core], w_sems.at[row], to_x(d))
    for d in ZD:
        send(wr_ref.at[z], wr_ref.at[z], wz_sems.at[d - 1], to_z(d))

    for d in XD:
        arrive(kx_ref.at[d - 1], k_sems.at[d])
    ksum = ks_ref[x]
    for d in XD:
        ksum = ksum + kx_ref[d - 1]
    ks_ref[x] = ksum
    for d in YD:
        piece = ks_ref.at[x, lax.min(yp(d), NP - 1)]
        goes = yp(d) < NP

        @pl.when(goes)
        def _():
            send(piece, ky_ref.at[d - 1], k_sems.at[NX + d], to_y(d), goes)

    for d in YD:
        tile = wc_ref.at[x, yp(NY - d), core]
        sem = w_sems.at[at(x, yp(NY - d), core)]
        arrive(tile, sem)
        for dx in XD:
            send(tile, tile, sem, to_x(dx))
    send(wc_ref.at[x, :, core], wc_ref.at[x, :, core], w_sems.at[TS + x], to_core)

    held = y < NP
    yy = lax.min(y, NP - 1)

    @pl.when(held)
    def _():
        ksum = ks_ref[x, yy]
        for d in YD:
            arrive(ky_ref.at[d - 1], k_sems.at[NX + d])
            ksum = ksum + ky_ref[d - 1]
        kf_ref[...] = ksum
        for d in ZD:
            send(kf_ref, kz_ref.at[d - 1], kz_sems.at[d - 1], to_z(d), held)

    for d in ZD:
        src_z = zp(NZ - d)
        arrive(g_ref.at[src_z, core], gz_sems.at[d - 1])
    send(g_ref.at[:, core], g_ref.at[:, core], g_sems.at[NX + NY], to_core)

    for dx in XD:
        xb = xp(NX - dx)
        for dy in [0] + YD:
            arrive(wc_ref.at[xb, yp(NY - dy), core], w_sems.at[at(xb, yp(NY - dy), core)])
        send(wc_ref.at[xb, :, core], wc_ref.at[xb, :, core], w_sems.at[TS + xb], to_core)

    own_k = k_ref.at[core, x, yy]
    @pl.when(held)
    def _():
        ksum = kf_ref[...]
        for d in ZD:
            arrive(kz_ref.at[d - 1], kz_sems.at[d - 1])
            ksum = ksum + kz_ref[d - 1]
        k_ref[core, x, yy] = ksum
        for d in YD:
            send(own_k, own_k, ka_sems.at[d], to_y(d), held)

    for d in YD:
        src_y = yp(NY - d)

        @pl.when(src_y < NP)
        def _():
            piece = k_ref.at[core, x, lax.min(src_y, NP - 1)]
            arrive(piece, ka_sems.at[d])
    for d in XD:
        send(k_ref.at[core, x], k_ref.at[core, x], ka_sems.at[NY + d], to_x(d))
    for d in XD:
        arrive(k_ref.at[core, xp(NX - d)], ka_sems.at[NY + d])
    send(k_ref.at[core], k_ref.at[core], ka_sems.at[0], to_core)

    for d in ZD:
        arrive(wr_ref.at[zp(NZ - d)], wz_sems.at[d - 1])
    arrive(g_ref.at[:, other], g_sems.at[NX + NY])
    for dx in [0] + XD:
        xb = xp(NX - dx)
        arrive(wc_ref.at[xb, :, other], w_sems.at[TS + xb])
    arrive(k_ref.at[other], ka_sems.at[0])
    for slot, (src, when) in enumerate(sent):
        if when is None:
            left(slot, src)
        else:
            pl.when(when)(functools.partial(left, slot, src))


def exchange(matrix, panel, sizes):
    NX, NY, NZ, TR, WIDTH, PW = sizes
    f32 = jnp.float32
    TS = NX * NY * 2
    NP = PW // 2 // NX // 8
    GR = PW // NZ // 2
    vmem = pl.BlockSpec(memory_space=pltpu.VMEM)
    shape = lambda *s: jax.ShapeDtypeStruct(s, f32)
    V = lambda *s: pltpu.VMEM(s, f32)
    D = lambda n: pltpu.SemaphoreType.DMA((n,))
    return pl.pallas_call(
        functools.partial(comm_kernel, sizes),
        out_shape=[shape(NZ, 2, GR, PW), shape(2, NX, NP, 8, PW), shape(NX, NY, 2, TR, PW),
                   shape(NX, NY, 2, TR, PW), shape(NZ, TR, PW)],
        in_specs=[vmem, vmem],
        out_specs=[vmem] * 5,
        scratch_shapes=[
            V(NZ, TR, WIDTH), V(NZ, 2, GR, PW), V(GR, PW), V(GR, PW), V(NX - 1, GR, PW), V(GR, PW),
            V(NY - 1, GR, PW), V(GR, PW),
            V(NX, NY, 2, TR, PW), V(NX, NY, TR, PW), V(NX - 1, NY, TR, PW), V(NX, NY, TR, PW),
            V(NY - 1, TR, PW),
            V(NZ, TR, PW), V(NZ - 1, TR, PW), V(2, NX, NP, 8, PW), V(NX, NP, 8, PW),
            V(NX - 1, NP, 8, PW), V(NX, NP, 8, PW), V(NY - 1, 8, PW), V(NZ - 1, 8, PW), V(8, PW),
            D(200), D(TS + NX), D(TS + NX), D(NZ - 1), D(NX), D(NX - 1), D(NY - 1), D(NZ - 1),
            D(NX + NY + 1), D(NZ - 1), D(NX + NY), D(NZ - 1), D(NX + NY),
        ],
        compiler_params=pltpu.CompilerParams(
            collective_id=0, has_side_effects=True, vmem_limit_bytes=32 * 2**20),
        name="exchange",
    )(matrix, panel)


def inverse(gram):
    n = gram.shape[0]
    ids_r = lax.broadcasted_iota(jnp.int32, (n, n), 0)
    ids_c = lax.broadcasted_iota(jnp.int32, (n, n), 1)
    eye = jnp.where(ids_r == ids_c, 1.0, 0.0)
    diag = gram * eye
    s_row = lax.rsqrt(jnp.sum(diag, axis=0, keepdims=True))
    s_col = lax.rsqrt(jnp.sum(diag, axis=1, keepdims=True))
    scaled = gram * s_row * s_col
    bound = jnp.max(jnp.sum(jnp.abs(scaled), axis=0, keepdims=True))
    start = eye * (2.0 / (1.0 + bound))

    def step(state):
        count, _, guess = state
        residual = eye - dot_nn(scaled, guess)
        error = jnp.sum(residual * residual)
        return count + 1, error, guess + dot_nn(guess, residual)

    def again(state):
        return jnp.logical_and(state[1] > 1e-8, state[0] < 80)

    _, _, found = lax.while_loop(again, step, (0, jnp.float32(1.0), start))
    return found * s_row * s_col


def finish_kernel(mat_ref, pan_ref, g_ref, k_ref, tc_ref, wc_ref, wr_ref, out_ref):
    NZ, TR, WIDTH = mat_ref.shape
    PW = pan_ref.shape[2]
    row = lax.axis_index("row")
    z = lax.axis_index("col")
    inv = inverse(g_ref[...])
    half = k_ref[...]
    proj = half + half.T
    t_rows = pan_ref[...].reshape(NZ * TR, PW)
    w_rows = wr_ref[...].reshape(NZ * TR, PW)
    left = dot_nn(t_rows, inv)
    right = dot_nn(w_rows - 2.0 * dot_nn(left, proj), inv)
    sub = lax.broadcasted_iota(jnp.int32, (TR, WIDTH), 0) + row * TR
    lane = lax.broadcasted_iota(jnp.int32, (TR, WIDTH), 1)
    change = dot_nt(left, wc_ref[...]) + dot_nt(right, tc_ref[...])
    change = change.reshape(NZ, TR, WIDTH)
    for a in range(NZ):
        new = mat_ref[a] - 2.0 * change[a]
        keep = jnp.logical_or(z < a, jnp.logical_and(z == a, sub >= lane))
        out_ref[a] = jnp.where(keep, new, 0.0)


def finish(matrix, panel, gram, proj, t_cols, w_cols, w_rows):
    vmem = pl.BlockSpec(memory_space=pltpu.VMEM)
    return pl.pallas_call(
        finish_kernel,
        out_shape=jax.ShapeDtypeStruct(matrix.shape, jnp.float32),
        in_specs=[vmem] * 7,
        out_specs=vmem,
        compiler_params=pltpu.CompilerParams(vmem_limit_bytes=32 * 2**20),
        name="finish",
    )(matrix, panel, gram, proj, t_cols, w_cols, w_rows)


def per_device(matrix, panel):
    NZ, _, TR, WIDTH = matrix.shape
    PW = panel.shape[3]
    NX, NY = PLANES[lax.axis_size("row")]
    sizes = (NX, NY, NZ, TR, WIDTH, PW)
    mat = matrix.reshape(NZ, TR, WIDTH)
    pan = panel.reshape(NZ, TR, PW)
    gram, proj, t_cols, w_cols, w_rows = exchange(mat, pan, sizes)
    out = finish(mat, pan, gram.reshape(PW, PW), proj.reshape(PW, PW),
                 t_cols.reshape(WIDTH, PW), w_cols.reshape(WIDTH, PW), w_rows)
    return out.reshape(NZ, 1, TR, WIDTH)


def solution(mesh):
    in_specs = (P(None, "row", None, "col"), P(None, "row", None, None))
    out_specs = P(None, "row", None, "col")
    return jax.shard_map(
        per_device, mesh=mesh, in_specs=in_specs, out_specs=out_specs, check_vma=False)
```

```python
import functools

import jax
import jax.numpy as jnp
from jax import lax
from jax.experimental import pallas as pl
from jax.experimental.pallas import tpu as pltpu
from jax.sharding import PartitionSpec as P

EXACT = lax.Precision.HIGHEST
PLANES = {64: (4, 8), 8: (2, 2)}


def dot_nn(a, b):
    return lax.dot_general(a, b, (((1,), (0,)), ((), ())), precision=EXACT,
                           preferred_element_type=jnp.float32)


def dot_tn(a, b):
    return lax.dot_general(a, b, (((0,), (0,)), ((), ())), precision=EXACT,
                           preferred_element_type=jnp.float32)


def dot_nt(a, b):
    return lax.dot_general(a, b, (((1,), (1,)), ((), ())), precision=EXACT,
                           preferred_element_type=jnp.float32)


def two_parts(a):
    high = a.astype(jnp.bfloat16)
    return high, (a - high.astype(jnp.float32)).astype(jnp.bfloat16)


def dot_split(a, b, dims):
    ah, al = two_parts(a)
    bh, bl = two_parts(b)
    dot = lambda p, q: lax.dot_general(p, q, (dims, ((), ())), preferred_element_type=jnp.float32)
    return dot(ah, bh) + (dot(ah, bl) + dot(al, bh))


NN, TN, NT = ((1,), (0,)), ((0,), (0,)), ((1,), (1,))


def by_distance(n):
    return sorted(range(1, n), key=lambda d: (min(d, n - d), d))


def scaled_gram(gram):
    n = gram.shape[0]
    eye = jnp.where(lax.broadcasted_iota(jnp.int32, (n, n), 0)
                    == lax.broadcasted_iota(jnp.int32, (n, n), 1), 1.0, 0.0)
    diag = gram * eye
    s_row = lax.rsqrt(jnp.sum(diag, axis=0, keepdims=True))
    s_col = lax.rsqrt(jnp.sum(diag, axis=1, keepdims=True))
    scaled = gram * s_row * s_col
    bound = jnp.max(jnp.sum(jnp.abs(scaled), axis=0, keepdims=True))
    return scaled, eye, s_row, s_col, eye * (2.0 / (1.0 + bound))


FIXED_STEPS = 7


def comm_kernel(sizes, mat_hbm, pan_hbm, g_ref, k_ref, tc_ref, wc_ref, wr_ref, inv_ref, err_ref,
                mat_ref, pan_ref, sg_ref,
                h_ref, gl_ref, gc_ref, gsum_ref, gx_ref, gsx_ref, gy_ref, gf_ref,
                mp_ref, cx_ref, mx_ref, ms_ref, my_ref,
                dp_ref, rz_ref, kp_ref, kc_ref, kx_ref, ks_ref, ky_ref, kz_ref, kf_ref,
                in_sems,
                send_sems, t_sems, w_sems, wz_sems, mc_sems, mx_sems, my_sems, dz_sems,
                g_sems, gz_sems, k_sems, kz_sems, ka_sems):
    NX, NY, NZ, TR, WIDTH, PW = sizes
    TS = NX * NY * 2
    NP = PW // 2 // NX // 8
    row = lax.axis_index("row")
    z = lax.axis_index("col")
    core = lax.rem(row, 2)
    chip = lax.div(row, 2)
    y = lax.rem(chip, NY)
    x = lax.div(chip, NY)
    other = 1 - core

    def at(x_, y_, c_):
        return (x_ * NY + y_) * 2 + c_

    def xp(d):
        return lax.rem(x + d, NX)

    def yp(d):
        return lax.rem(y + d, NY)

    def zp(d):
        return lax.rem(z + d, NZ)

    to_x = lambda d: (at(xp(d), y, core), z)
    to_y = lambda d: (at(x, yp(d), core), z)
    to_z = lambda d: (row, zp(d))
    to_core = (at(x, y, other), z)

    barrier = pltpu.get_barrier_semaphore()
    peers = ([to_x(d) for d in range(1, NX)] + [to_y(d) for d in range(1, NY)]
             + [to_z(d) for d in range(1, NZ)] + [to_core])
    for peer in peers:
        pl.semaphore_signal(barrier, inc=1, device_id=peer, device_id_type=pl.DeviceIdType.MESH)

    pan_in = pltpu.make_async_copy(pan_hbm, pan_ref, in_sems.at[0])
    mat_in = pltpu.make_async_copy(mat_hbm, mat_ref, in_sems.at[1])
    pan_in.start()
    mat_in.start()

    sent = []

    def send(src, dst, sem, peer, when=None):
        slot = len(sent)
        sent.append((src, when))
        pltpu.make_async_remote_copy(
            src_ref=src, dst_ref=dst, send_sem=send_sems.at[slot], recv_sem=sem,
            device_id=peer, device_id_type=pl.DeviceIdType.MESH).start()

    def left(slot, src):
        pltpu.make_async_remote_copy(
            src_ref=src, dst_ref=src, send_sem=send_sems.at[slot], recv_sem=t_sems.at[0],
            device_id=to_core, device_id_type=pl.DeviceIdType.MESH).wait_send()

    def arrive(dst, sem):
        pltpu.make_async_remote_copy(
            src_ref=dst, dst_ref=dst, send_sem=send_sems.at[0], recv_sem=sem,
            device_id=to_core, device_id_type=pl.DeviceIdType.MESH).wait_recv()

    YD, XD, ZD = by_distance(NY), by_distance(NX), by_distance(NZ)

    pan_in.wait()
    tc_ref[x, y, core] = pan_ref[z]
    t_rows = pan_ref[...].reshape(NZ * TR, PW)
    gl_ref[...] = dot_tn(t_rows, t_rows).reshape(NZ, 2, PW // NZ // 2, PW)
    mat_in.wait()
    sub = lax.broadcasted_iota(jnp.int32, (TR, WIDTH), 0) + row * TR
    lane = lax.broadcasted_iota(jnp.int32, (TR, WIDTH), 1)
    for a in range(NZ):
        tile = mat_ref[a]
        diag_part = jnp.where(sub > lane, tile, jnp.where(sub == lane, 0.5 * tile, 0.0))
        h_ref[a] = jnp.where(z < a, tile, jnp.where(z == a, diag_part, 0.0))
    XW = WIDTH // NX
    for d in list(XD) + [0]:
        xb = xp(d)
        cols = pl.ds(pl.multiple_of(xb * XW, XW), XW)
        h = h_ref[:, :, cols].reshape(NZ * TR, XW)
        mp_ref[xb] = dot_tn(h, t_rows).reshape(NY, 2, TR, PW)
    pl.semaphore_wait(barrier, len(peers))

    own_t = pan_ref.at[z]
    for d in YD:
        send(own_t, tc_ref.at[x, y, core], t_sems.at[row], to_y(d))
    for d in XD:
        send(own_t, tc_ref.at[x, y, core], t_sems.at[row], to_x(d))
    send(gl_ref.at[z, other], gc_ref, g_sems.at[0], to_core)
    for d in list(XD) + [0]:
        send(mp_ref.at[xp(d), :, other], cx_ref.at[xp(d)], mc_sems.at[xp(d)], to_core)

    arrive(gc_ref, g_sems.at[0])
    gsum_ref[...] = gl_ref[z, core] + gc_ref[...]
    for d in XD:
        send(gsum_ref, gx_ref.at[d - 1], g_sems.at[d], to_x(d))

    for d in YD:
        tile = tc_ref.at[x, yp(NY - d), core]
        sem = t_sems.at[at(x, yp(NY - d), core)]
        arrive(tile, sem)
        for dx in XD:
            send(tile, tile, sem, to_x(dx))
    send(tc_ref.at[x, :, core], tc_ref.at[x, :, core], t_sems.at[TS + x], to_core)

    gs = gsum_ref[...]
    for d in XD:
        arrive(gx_ref.at[d - 1], g_sems.at[d])
        gs = gs + gx_ref[d - 1]
    gsx_ref[...] = gs
    for d in YD:
        send(gsx_ref, gy_ref.at[d - 1], g_sems.at[NX + d], to_y(d))

    for d in list(XD) + [0]:
        xb = xp(d)
        arrive(cx_ref.at[xb], mc_sems.at[xb])
        ms_ref[xb] = mp_ref[xb, :, core] + cx_ref[xb]
        if d:
            send(ms_ref.at[xb], mx_ref.at[d - 1], mx_sems.at[d - 1], to_x(d))

    for dx in XD:
        xb = xp(NX - dx)
        for dy in [0] + YD:
            arrive(tc_ref.at[xb, yp(NY - dy), core], t_sems.at[at(xb, yp(NY - dy), core)])
        send(tc_ref.at[xb, :, core], tc_ref.at[xb, :, core], t_sems.at[TS + xb], to_core)

    gs = gsx_ref[...]
    for d in YD:
        arrive(gy_ref.at[d - 1], g_sems.at[NX + d])
        gs = gs + gy_ref[d - 1]
    gf_ref[...] = gs
    g_ref[z, core] = gs
    for d in ZD:
        send(gf_ref, g_ref.at[z, core], gz_sems.at[d - 1], to_z(d))

    for dx in [0] + XD:
        xb = xp(NX - dx)
        arrive(tc_ref.at[xb, :, other], t_sems.at[TS + xb])

    direct = dot_split(h_ref[...].reshape(NZ * TR, WIDTH), tc_ref[...].reshape(WIDTH, PW), NN)
    dp_ref[...] = direct.reshape(NZ, TR, PW)
    for d in ZD:
        send(dp_ref.at[zp(d)], rz_ref.at[d - 1], dz_sems.at[d - 1], to_z(d))
    kp_ref[...] = dot_split(t_rows, direct, TN).reshape(2, NX, NP, 8, PW)
    send(kp_ref.at[other], kc_ref, k_sems.at[0], to_core)

    msum = ms_ref[x]
    for d in XD:
        arrive(mx_ref.at[d - 1], mx_sems.at[d - 1])
        msum = msum + mx_ref[d - 1]
    mp_ref[x, :, core] = msum
    for d in YD:
        send(mp_ref.at[x, yp(d), core], my_ref.at[d - 1], my_sems.at[d - 1], to_y(d))

    arrive(kc_ref, k_sems.at[0])
    ks_ref[...] = kp_ref[core] + kc_ref[...]
    for d in XD:
        send(ks_ref.at[xp(d)], kx_ref.at[d - 1], k_sems.at[d], to_x(d))

    msum = mp_ref[x, y, core]
    for d in YD:
        arrive(my_ref.at[d - 1], my_sems.at[d - 1])
        msum = msum + my_ref[d - 1]

    for d in ZD:
        arrive(g_ref.at[zp(NZ - d), core], gz_sems.at[d - 1])
    send(g_ref.at[:, core], g_ref.at[:, core], g_sems.at[NX + NY], to_core)

    ksum = ks_ref[x]
    for d in XD:
        arrive(kx_ref.at[d - 1], k_sems.at[d])
        ksum = ksum + kx_ref[d - 1]
    ks_ref[x] = ksum
    for d in YD:
        piece = ks_ref.at[x, lax.min(yp(d), NP - 1)]
        goes = yp(d) < NP

        @pl.when(goes)
        def _():
            send(piece, ky_ref.at[d - 1], k_sems.at[NX + d], to_y(d), goes)

    wsum = msum + dp_ref[z]
    for d in ZD:
        arrive(rz_ref.at[d - 1], dz_sems.at[d - 1])
        wsum = wsum + rz_ref[d - 1]
    wc_ref[x, y, core] = wsum
    wr_ref[z] = wsum
    for d in YD:
        send(wc_ref.at[x, y, core], wc_ref.at[x, y, core], w_sems.at[row], to_y(d))
    for d in XD:
        send(wc_ref.at[x, y, core], wc_ref.at[x, y, core], w_sems.at[row], to_x(d))

    held = y < NP
    yy = lax.min(y, NP - 1)

    @pl.when(held)
    def _():
        ksum = ks_ref[x, yy]
        for d in YD:
            arrive(ky_ref.at[d - 1], k_sems.at[NX + d])
            ksum = ksum + ky_ref[d - 1]
        kf_ref[...] = ksum
        for d in ZD:
            send(kf_ref, kz_ref.at[d - 1], kz_sems.at[d - 1], to_z(d), held)

    for d in ZD:
        send(wr_ref.at[z], wr_ref.at[z], wz_sems.at[d - 1], to_z(d))

    arrive(g_ref.at[:, other], g_sems.at[NX + NY])
    scaled, eye, s_row, s_col, start = scaled_gram(g_ref[...].reshape(PW, PW))
    sg_ref[...] = scaled
    inv_ref[...] = start

    def newton(count):
        for _ in range(count):
            residual = eye - dot_split(sg_ref[...], inv_ref[...], NN)
            inv_ref[...] += dot_split(inv_ref[...], residual, NN)

    newton(1)

    for d in YD:
        tile = wc_ref.at[x, yp(NY - d), core]
        sem = w_sems.at[at(x, yp(NY - d), core)]
        arrive(tile, sem)
        for dx in XD:
            send(tile, tile, sem, to_x(dx))
    send(wc_ref.at[x, :, core], wc_ref.at[x, :, core], w_sems.at[TS + x], to_core)
    newton(2)

    own_k = k_ref.at[core, x, yy]

    @pl.when(held)
    def _():
        ksum = kf_ref[...]
        for d in ZD:
            arrive(kz_ref.at[d - 1], kz_sems.at[d - 1])
            ksum = ksum + kz_ref[d - 1]
        k_ref[core, x, yy] = ksum
        for d in YD:
            send(own_k, own_k, ka_sems.at[d], to_y(d), held)

    for dx in XD:
        xb = xp(NX - dx)
        for dy in [0] + YD:
            arrive(wc_ref.at[xb, yp(NY - dy), core], w_sems.at[at(xb, yp(NY - dy), core)])
        send(wc_ref.at[xb, :, core], wc_ref.at[xb, :, core], w_sems.at[TS + xb], to_core)
    newton(2)

    for d in YD:
        src_y = yp(NY - d)

        @pl.when(src_y < NP)
        def _():
            piece = k_ref.at[core, x, lax.min(src_y, NP - 1)]
            arrive(piece, ka_sems.at[d])
    for d in XD:
        send(k_ref.at[core, x], k_ref.at[core, x], ka_sems.at[NY + d], to_x(d))
    newton(FIXED_STEPS - 5)
    for d in XD:
        arrive(k_ref.at[core, xp(NX - d)], ka_sems.at[NY + d])
    send(k_ref.at[core], k_ref.at[core], ka_sems.at[0], to_core)

    residual = eye - dot_nn(sg_ref[...], inv_ref[...])
    err_ref[...] = jnp.full(err_ref.shape, jnp.sum(residual * residual), jnp.float32)
    inv_ref[...] += dot_split(inv_ref[...], residual, NN)

    for d in ZD:
        arrive(wr_ref.at[zp(NZ - d)], wz_sems.at[d - 1])
    for dx in [0] + XD:
        xb = xp(NX - dx)
        arrive(wc_ref.at[xb, :, other], w_sems.at[TS + xb])
    arrive(k_ref.at[other], ka_sems.at[0])
    for slot, (src, when) in enumerate(sent):
        if when is None:
            left(slot, src)
        else:
            pl.when(when)(functools.partial(left, slot, src))


def exchange(matrix, panel, sizes):
    NX, NY, NZ, TR, WIDTH, PW = sizes
    f32 = jnp.float32
    TS = NX * NY * 2
    NP = PW // 2 // NX // 8
    GR = PW // NZ // 2
    vmem = pl.BlockSpec(memory_space=pltpu.VMEM)
    shape = lambda *s: jax.ShapeDtypeStruct(s, f32)
    V = lambda *s: pltpu.VMEM(s, f32)
    D = lambda n: pltpu.SemaphoreType.DMA((n,))
    return pl.pallas_call(
        functools.partial(comm_kernel, sizes),
        out_shape=[shape(NZ, 2, GR, PW), shape(2, NX, NP, 8, PW), shape(NX, NY, 2, TR, PW),
                   shape(NX, NY, 2, TR, PW), shape(NZ, TR, PW), shape(PW, PW), shape(8, 128)],
        in_specs=[pl.BlockSpec(memory_space=pl.ANY)] * 2,
        out_specs=[vmem] * 7,
        scratch_shapes=[
            V(NZ, TR, WIDTH), V(NZ, TR, PW), V(PW, PW),
            V(NZ, TR, WIDTH), V(NZ, 2, GR, PW), V(GR, PW), V(GR, PW), V(NX - 1, GR, PW), V(GR, PW),
            V(NY - 1, GR, PW), V(GR, PW),
            V(NX, NY, 2, TR, PW), V(NX, NY, TR, PW), V(NX - 1, NY, TR, PW), V(NX, NY, TR, PW),
            V(NY - 1, TR, PW),
            V(NZ, TR, PW), V(NZ - 1, TR, PW), V(2, NX, NP, 8, PW), V(NX, NP, 8, PW),
            V(NX - 1, NP, 8, PW), V(NX, NP, 8, PW), V(NY - 1, 8, PW), V(NZ - 1, 8, PW), V(8, PW),
            D(2), D(200), D(TS + NX), D(TS + NX), D(NZ - 1), D(NX), D(NX - 1), D(NY - 1), D(NZ - 1),
            D(NX + NY + 1), D(NZ - 1), D(NX + NY), D(NZ - 1), D(NX + NY),
        ],
        compiler_params=pltpu.CompilerParams(
            collective_id=0, has_side_effects=True, vmem_limit_bytes=32 * 2**20),
        name="exchange",
    )(matrix, panel)


def polish(gram, guess, error):
    scaled, eye, s_row, s_col, start = scaled_gram(gram)
    usable = error < 0.25

    def step(state):
        count, _, guess = state
        residual = eye - dot_nn(scaled, guess)
        error = jnp.sum(residual * residual)
        return count + 1, error, guess + dot_nn(guess, residual)

    def again(state):
        return jnp.logical_and(state[1] > 1e-8, state[0] < 80)

    state = (0, jnp.where(usable, error, 1.0), jnp.where(usable, guess, start))
    _, _, found = lax.while_loop(again, step, state)
    return found * s_row * s_col


def finish_kernel(mat_ref, pan_ref, g_ref, k_ref, tc_ref, wc_ref, wr_ref, inv_ref, err_ref, out_ref):
    NZ, TR, WIDTH = mat_ref.shape
    PW = pan_ref.shape[2]
    row = lax.axis_index("row")
    z = lax.axis_index("col")
    inv = polish(g_ref[...], inv_ref[...], err_ref[0, 0])
    half = k_ref[...]
    proj = half + half.T
    t_rows = pan_ref[...].reshape(NZ * TR, PW)
    w_rows = wr_ref[...].reshape(NZ * TR, PW)
    left = dot_nn(t_rows, inv)
    right = dot_nn(w_rows - 2.0 * dot_nn(left, proj), inv)
    sub = lax.broadcasted_iota(jnp.int32, (TR, WIDTH), 0) + row * TR
    lane = lax.broadcasted_iota(jnp.int32, (TR, WIDTH), 1)
    change = dot_split(left, wc_ref[...], NT) + dot_split(right, tc_ref[...], NT)
    change = change.reshape(NZ, TR, WIDTH)
    for a in range(NZ):
        new = mat_ref[a] - 2.0 * change[a]
        keep = jnp.logical_or(z < a, jnp.logical_and(z == a, sub >= lane))
        out_ref[a] = jnp.where(keep, new, 0.0)


def finish(*operands):
    matrix = operands[0]
    vmem = pl.BlockSpec(memory_space=pltpu.VMEM)
    return pl.pallas_call(
        finish_kernel,
        out_shape=jax.ShapeDtypeStruct(matrix.shape, jnp.float32),
        in_specs=[vmem] * len(operands),
        out_specs=vmem,
        compiler_params=pltpu.CompilerParams(vmem_limit_bytes=32 * 2**20),
        name="finish",
    )(*operands)


def per_device(matrix, panel):
    NZ, _, TR, WIDTH = matrix.shape
    PW = panel.shape[3]
    NX, NY = PLANES[lax.axis_size("row")]
    sizes = (NX, NY, NZ, TR, WIDTH, PW)
    mat = matrix.reshape(NZ, TR, WIDTH)
    pan = panel.reshape(NZ, TR, PW)
    gram, proj, t_cols, w_cols, w_rows, guess, error = exchange(mat, pan, sizes)
    out = finish(mat, pan, gram.reshape(PW, PW), proj.reshape(PW, PW),
                 t_cols.reshape(WIDTH, PW), w_cols.reshape(WIDTH, PW), w_rows, guess, error)
    return out.reshape(NZ, 1, TR, WIDTH)


def solution(mesh):
    in_specs = (P(None, "row", None, "col"), P(None, "row", None, None))
    out_specs = P(None, "row", None, "col")
    return jax.shard_map(
        per_device, mesh=mesh, in_specs=in_specs, out_specs=out_specs, check_vma=False)
```

```python
import functools

import jax
import jax.numpy as jnp
from jax import lax
from jax.experimental import pallas as pl
from jax.experimental.pallas import tpu as pltpu
from jax.sharding import PartitionSpec as P

EXACT = lax.Precision.HIGHEST
PLANES = {64: (4, 8), 8: (2, 2)}


def dot_nn(a, b):
    return lax.dot_general(a, b, (((1,), (0,)), ((), ())), precision=EXACT,
                           preferred_element_type=jnp.float32)


def dot_tn(a, b):
    return lax.dot_general(a, b, (((0,), (0,)), ((), ())), precision=EXACT,
                           preferred_element_type=jnp.float32)


def dot_nt(a, b):
    return lax.dot_general(a, b, (((1,), (1,)), ((), ())), precision=EXACT,
                           preferred_element_type=jnp.float32)


def two_parts(a):
    high = a.astype(jnp.bfloat16)
    return high, (a - high.astype(jnp.float32)).astype(jnp.bfloat16)


def dot_split(a, b, dims):
    ah, al = two_parts(a)
    bh, bl = two_parts(b)
    dot = lambda p, q: lax.dot_general(p, q, (dims, ((), ())), preferred_element_type=jnp.float32)
    return dot(ah, bh) + (dot(ah, bl) + dot(al, bh))


NN, TN, NT = ((1,), (0,)), ((0,), (0,)), ((1,), (1,))


def by_distance(n):
    return sorted(range(1, n), key=lambda d: (min(d, n - d), d))


def scaled_gram(gram):
    n = gram.shape[0]
    eye = jnp.where(lax.broadcasted_iota(jnp.int32, (n, n), 0)
                    == lax.broadcasted_iota(jnp.int32, (n, n), 1), 1.0, 0.0)
    diag = gram * eye
    s_row = lax.rsqrt(jnp.sum(diag, axis=0, keepdims=True))
    s_col = lax.rsqrt(jnp.sum(diag, axis=1, keepdims=True))
    scaled = gram * s_row * s_col
    bound = jnp.max(jnp.sum(jnp.abs(scaled), axis=0, keepdims=True))
    return scaled, eye, s_row, s_col, eye * (2.0 / (1.0 + bound))


COARSE_STEPS = 4


def comm_kernel(sizes, mat_hbm, pan_hbm, g_ref, k_ref, tc_ref, wc_ref, wr_ref, inv_ref, err_ref,
                mat_ref, pan_ref, sg_ref, units_ref, h_ref,
                gl_ref, gc_ref, gsum_ref, gx_ref, gsx_ref, gy_ref,
                mpa_ref, mpb_ref, ca_ref, cb_ref, ax_ref, ay_ref, by_ref, bs_ref, bx_ref,
                dp_ref, rz_ref, kp_ref, kc_ref, kx_ref, ks_ref, ky_ref, kz_ref, kf_ref,
                in_sems, out_sems, ky_out_sems, t_sems, w_sems, wz_sems, ma_sems, mb_sems, dz_sems,
                g_sems, gz_sems, ga_sems, k_sems, kz_sems, ka_sems):
    NX, NY, NZ, TR, WIDTH, PW, NL, LA = sizes
    NP = PW // 2 // NX // 8
    LW = PW // NL
    row = lax.axis_index("row")
    z = lax.axis_index("col")
    core = lax.rem(row, 2)
    chip = lax.div(row, 2)
    y = lax.rem(chip, NY)
    x = lax.div(chip, NY)
    other = 1 - core

    def at(x_, y_, c_):
        return (x_ * NY + y_) * 2 + c_

    def xp(d):
        return lax.rem(x + d, NX)

    def yp(d):
        return lax.rem(y + d, NY)

    def zp(d):
        return lax.rem(z + d, NZ)

    to_x = lambda d: (at(xp(d), y, core), z)
    to_y = lambda d: (at(x, yp(d), core), z)
    to_z = lambda d: (row, zp(d))
    to_core = (at(x, y, other), z)

    barrier = pltpu.get_barrier_semaphore()
    peers = ([to_x(d) for d in range(1, NX)] + [to_y(d) for d in range(1, NY)]
             + [to_z(d) for d in range(1, NZ)] + [to_core])
    for peer in peers:
        pl.semaphore_signal(barrier, inc=1, device_id=peer, device_id_type=pl.DeviceIdType.MESH)

    pan_in = pltpu.make_async_copy(pan_hbm, pan_ref, in_sems.at[0])
    mat_in = pltpu.make_async_copy(mat_hbm, mat_ref, in_sems.at[1])
    pan_in.start()
    mat_in.start()

    totals = {}

    def send(src, dst, sem, peer, out):
        words = 1
        for n in src.shape:
            words *= n
        totals[out] = totals.get(out, 0) + words
        pltpu.make_async_remote_copy(
            src_ref=src, dst_ref=dst, send_sem=out_sems.at[out], recv_sem=sem,
            device_id=peer, device_id_type=pl.DeviceIdType.MESH).start()

    def left(ref, sem):
        pltpu.make_async_remote_copy(
            src_ref=ref, dst_ref=ref, send_sem=sem, recv_sem=t_sems.at[0],
            device_id=to_core, device_id_type=pl.DeviceIdType.MESH).wait_send()

    def all_left(out):
        assert totals[out] % (8 * PW) == 0
        left(units_ref.at[pl.ds(0, totals[out] // (8 * PW))], out_sems.at[out])

    def arrive(dst, sem):
        pltpu.make_async_remote_copy(
            src_ref=dst, dst_ref=dst, send_sem=out_sems.at[0], recv_sem=sem,
            device_id=to_core, device_id_type=pl.DeviceIdType.MESH).wait_recv()

    OUT_T, OUT_W, OUT_MA, OUT_MB, OUT_D, OUT_K, OUT_KZ, OUT_KY, OUT_G, OUT_GS, OUT_GX, OUT_GC = range(12)
    YD, XD, ZD = by_distance(NY), by_distance(NX), by_distance(NZ)

    pan_in.wait()
    tc_ref[x, y, core] = pan_ref[z]
    t_rows = pan_ref[...].reshape(NZ * TR, PW)
    gram = dot_tn(t_rows, t_rows)
    for l in range(NL):
        gl_ref[l] = gram[:, l * LW:(l + 1) * LW].reshape(NZ, 2, PW // NZ // 2, LW)
    mat_in.wait()
    sub = lax.broadcasted_iota(jnp.int32, (TR, WIDTH), 0) + row * TR
    lane = lax.broadcasted_iota(jnp.int32, (TR, WIDTH), 1)
    for a in range(NZ):
        tile = mat_ref[a]
        diag_part = jnp.where(sub > lane, tile, jnp.where(sub == lane, 0.5 * tile, 0.0))
        h_ref[a] = jnp.where(z < a, tile, jnp.where(z == a, diag_part, 0.0))
    XW = WIDTH // NX

    def columns(xb):
        return h_ref[:, :, pl.ds(pl.multiple_of(xb * XW, XW), XW)].reshape(NZ * TR, XW)

    for d in [0] + XD:
        xb = xp(d)
        terms = dot_tn(columns(xb), t_rows).reshape(NY, 2, TR, PW)
        for c in range(2):
            mpa_ref[c, xb] = terms[:, c, :, :LA]
            mpb_ref[c, :, xb] = terms[:, c, :, LA:]
    pl.semaphore_wait(barrier, len(peers))

    own_t = pan_ref.at[z]
    for d in YD:
        send(own_t, tc_ref.at[x, y, core], t_sems.at[d], to_y(d), OUT_T)
    for d in XD:
        send(own_t, tc_ref.at[x, y, core], t_sems.at[NY + d], to_x(d), OUT_T)
    send(gl_ref.at[:, z, other], gc_ref, g_sems.at[0], to_core, OUT_G)
    send(mpb_ref.at[other], cb_ref, mb_sems.at[0], to_core, OUT_MB)
    send(mpa_ref.at[other], ca_ref, ma_sems.at[0], to_core, OUT_MA)

    holds_g = x < NL
    own_l = lax.min(x, NL - 1)
    arrive(gc_ref, g_sems.at[0])
    gsum_ref[...] = gl_ref[:, z, core] + gc_ref[...]
    for d in XD:
        @pl.when(xp(d) < NL)
        def _():
            pltpu.make_async_remote_copy(
                src_ref=gsum_ref.at[lax.min(xp(d), NL - 1)], dst_ref=gx_ref.at[d - 1],
                send_sem=ky_out_sems.at[NY + d], recv_sem=g_sems.at[d],
                device_id=to_x(d), device_id_type=pl.DeviceIdType.MESH).start()

    def forward_t(ds):
        for d in ds:
            tile = tc_ref.at[x, yp(NY - d), core]
            arrive(tile, t_sems.at[d])
            for dx in XD:
                send(tile, tile, t_sems.at[NY + dx], to_x(dx), OUT_T)

    forward_t(YD[:3])

    @pl.when(holds_g)
    def _():
        gs = gsum_ref[own_l]
        for d in XD:
            arrive(gx_ref.at[d - 1], g_sems.at[d])
            gs = gs + gx_ref[d - 1]
        gsx_ref[...] = gs
        for d in YD:
            send(gsx_ref, gy_ref.at[d - 1], g_sems.at[NX + d], to_y(d), OUT_GS)

    arrive(cb_ref, mb_sems.at[0])
    mpb_ref[core] = mpb_ref[core] + cb_ref[...]
    for d in YD:
        send(mpb_ref.at[core, yp(d)], by_ref.at[d - 1], mb_sems.at[d], to_y(d), OUT_MB)

    forward_t(YD[3:])
    send(tc_ref.at[x, :, core], tc_ref.at[x, :, core], t_sems.at[NY + NX], to_core, OUT_T)
    arrive(ca_ref, ma_sems.at[0])
    mpa_ref[core] = mpa_ref[core] + ca_ref[...]

    def project(xb):
        tiles = tc_ref[xb, :, core].reshape(NY * TR, PW)
        return (dot_split(tiles, mpa_ref[core, xb].reshape(NY * TR, LA), TN),
                dot_split(tiles, mpb_ref[core, :, xb].reshape(NY * TR, PW - LA), TN))

    ka, kb = project(x)
    for dx in XD:
        xb = xp(NX - dx)
        arrive(tc_ref.at[xb, :, core], t_sems.at[NY + dx])
        send(tc_ref.at[xb, :, core], tc_ref.at[xb, :, core], t_sems.at[NY + NX + dx], to_core, OUT_T)
        more_a, more_b = project(xb)
        ka, kb = ka + more_a, kb + more_b
        if dx == XD[min(1, len(XD) - 1)]:
            @pl.when(holds_g)
            def _():
                gs = gsx_ref[...]
                for d in YD:
                    arrive(gy_ref.at[d - 1], g_sems.at[NX + d])
                    gs = gs + gy_ref[d - 1]
                g_ref[own_l, z, core] = gs
                own_g = g_ref.at[own_l, z, core]
                for d in ZD:
                    send(own_g, own_g, gz_sems.at[d - 1], to_z(d), OUT_GS)
    kp_ref[:, :, :, :, :LA] = ka.reshape(2, NX, NP, 8, LA)
    kp_ref[:, :, :, :, LA:] = kb.reshape(2, NX, NP, 8, PW - LA)
    send(kp_ref.at[other], kc_ref, k_sems.at[0], to_core, OUT_K)

    arrive(tc_ref.at[x, :, other], t_sems.at[NY + NX])
    direct = dot_split(columns(x), tc_ref[x].reshape(XW, PW), NN)

    arrive(kc_ref, k_sems.at[0])
    ks_ref[...] = kp_ref[core] + kc_ref[...]
    for d in XD:
        send(ks_ref.at[xp(d)], kx_ref.at[d - 1], k_sems.at[d], to_x(d), OUT_K)

    for dx in XD:
        xb = xp(NX - dx)
        arrive(tc_ref.at[xb, :, other], t_sems.at[NY + NX + dx])
        direct = direct + dot_split(columns(xb), tc_ref[xb].reshape(XW, PW), NN)
    dp_ref[...] = direct.reshape(NZ, TR, PW)
    for d in ZD:
        send(dp_ref.at[zp(d)], rz_ref.at[d - 1], dz_sems.at[d - 1], to_z(d), OUT_D)

    for d in XD:
        send(mpa_ref.at[core, xp(d)], ax_ref.at[d - 1], ma_sems.at[d], to_x(d), OUT_MA)

    ksum = ks_ref[x]
    for d in XD:
        arrive(kx_ref.at[d - 1], k_sems.at[d])
        ksum = ksum + kx_ref[d - 1]
    ks_ref[x] = ksum
    for d in YD:
        @pl.when(yp(d) < NP)
        def _():
            pltpu.make_async_remote_copy(
                src_ref=ks_ref.at[x, lax.min(yp(d), NP - 1)], dst_ref=ky_ref.at[d - 1],
                send_sem=ky_out_sems.at[d], recv_sem=k_sems.at[NX + d],
                device_id=to_y(d), device_id_type=pl.DeviceIdType.MESH).start()

    part = mpb_ref[core, y]
    for d in YD:
        arrive(by_ref.at[d - 1], mb_sems.at[d])
        part = part + by_ref[d - 1]
    bs_ref[...] = part
    for d in XD:
        send(bs_ref.at[xp(d)], bx_ref.at[d - 1], mb_sems.at[NY + d], to_x(d), OUT_MB)

    part = mpa_ref[core, x]
    for d in XD:
        arrive(ax_ref.at[d - 1], ma_sems.at[d])
        part = part + ax_ref[d - 1]
    mpa_ref[core, x] = part
    for d in YD:
        send(mpa_ref.at[core, x, yp(d)], ay_ref.at[d - 1], ma_sems.at[NX + d], to_y(d), OUT_MA)

    own_g = g_ref.at[own_l, :, core]

    @pl.when(holds_g)
    def _():
        for d in ZD:
            arrive(g_ref.at[own_l, zp(NZ - d), core], gz_sems.at[d - 1])
        for d in XD:
            send(own_g, own_g, ga_sems.at[d], to_x(d), OUT_GX)

    held = y < NP
    yy = lax.min(y, NP - 1)

    @pl.when(held)
    def _():
        ksum = ks_ref[x, yy]
        for d in YD:
            arrive(ky_ref.at[d - 1], k_sems.at[NX + d])
            ksum = ksum + ky_ref[d - 1]
        kf_ref[...] = ksum
        for d in ZD:
            send(kf_ref, kz_ref.at[d - 1], kz_sems.at[d - 1], to_z(d), OUT_KZ)

    part_b = bs_ref[x]
    for d in XD:
        arrive(bx_ref.at[d - 1], mb_sems.at[NY + d])
        part_b = part_b + bx_ref[d - 1]
    part_a = mpa_ref[core, x, y]
    for d in YD:
        arrive(ay_ref.at[d - 1], ma_sems.at[NX + d])
        part_a = part_a + ay_ref[d - 1]
    wsum = dp_ref[z]
    for d in ZD:
        arrive(rz_ref.at[d - 1], dz_sems.at[d - 1])
        wsum = wsum + rz_ref[d - 1]
    wr_ref[z, :, :LA] = wsum[:, :LA] + part_a
    wr_ref[z, :, LA:] = wsum[:, LA:] + part_b
    wc_ref[x, y, core] = wr_ref[z]
    own_w = wc_ref.at[x, y, core]
    for d in YD:
        send(own_w, own_w, w_sems.at[d], to_y(d), OUT_W)
    for d in XD:
        send(own_w, own_w, w_sems.at[NY + d], to_x(d), OUT_W)
    for d in ZD:
        send(wr_ref.at[z], wr_ref.at[z], wz_sems.at[d - 1], to_z(d), OUT_W)

    for d in XD:
        src_l = xp(NX - d)

        @pl.when(src_l < NL)
        def _():
            arrive(g_ref.at[lax.min(src_l, NL - 1), :, core], ga_sems.at[d])
    send(g_ref.at[:, :, core], g_ref.at[:, :, core], ga_sems.at[0], to_core, OUT_GC)

    arrive(g_ref.at[:, :, other], ga_sems.at[0])
    whole = jnp.concatenate([g_ref[l].reshape(PW, LW) for l in range(NL)], axis=1)
    scaled, eye, s_row, s_col, start = scaled_gram(whole)
    sg_ref[...] = scaled
    inv_ref[...] = start

    def newton(dot):
        residual = eye - dot(sg_ref[...], inv_ref[...])
        inv_ref[...] += dot(inv_ref[...], residual)

    coarse = lambda a, b: jnp.dot(a.astype(jnp.bfloat16), b.astype(jnp.bfloat16),
                                  preferred_element_type=jnp.float32)
    fine = lambda a, b: dot_split(a, b, NN)

    for n, d in enumerate(YD):
        tile = wc_ref.at[x, yp(NY - d), core]
        arrive(tile, w_sems.at[d])
        for dx in XD:
            send(tile, tile, w_sems.at[NY + dx], to_x(dx), OUT_W)
        if n < COARSE_STEPS:
            newton(coarse)
    send(wc_ref.at[x, :, core], wc_ref.at[x, :, core], w_sems.at[NY + NX], to_core, OUT_W)
    for _ in range(COARSE_STEPS - len(YD)):
        newton(coarse)

    own_k = k_ref.at[core, x, yy]

    @pl.when(held)
    def _():
        ksum = kf_ref[...]
        for d in ZD:
            arrive(kz_ref.at[d - 1], kz_sems.at[d - 1])
            ksum = ksum + kz_ref[d - 1]
        k_ref[core, x, yy] = ksum
        for d in YD:
            send(own_k, own_k, ka_sems.at[d], to_y(d), OUT_KY)
    newton(fine)
    newton(fine)

    def pass_w(dx):
        block = wc_ref.at[xp(NX - dx), :, core]
        arrive(block, w_sems.at[NY + dx])
        send(block, block, w_sems.at[NY + NX + dx], to_core, OUT_W)

    pass_w(XD[0])

    for d in YD:
        src_y = yp(NY - d)

        @pl.when(src_y < NP)
        def _():
            arrive(k_ref.at[core, x, lax.min(src_y, NP - 1)], ka_sems.at[d])
    for d in XD:
        send(k_ref.at[core, x], k_ref.at[core, x], ka_sems.at[NY + d], to_x(d), OUT_K)
    for dx in XD[1:]:
        pass_w(dx)
    newton(fine)
    for d in XD:
        arrive(k_ref.at[core, xp(NX - d)], ka_sems.at[NY + d])
    send(k_ref.at[core], k_ref.at[core], ka_sems.at[0], to_core, OUT_K)

    residual = eye - dot_nn(sg_ref[...], inv_ref[...])
    err_ref[...] = jnp.full(err_ref.shape, jnp.sum(residual * residual), jnp.float32)
    inv_ref[...] = (inv_ref[...] + fine(inv_ref[...], residual)) * s_row * s_col

    for d in ZD:
        arrive(wr_ref.at[zp(NZ - d)], wz_sems.at[d - 1])
    arrive(wc_ref.at[x, :, other], w_sems.at[NY + NX])
    for dx in XD:
        arrive(wc_ref.at[xp(NX - dx), :, other], w_sems.at[NY + NX + dx])
    arrive(k_ref.at[other], ka_sems.at[0])
    for out in (OUT_T, OUT_W, OUT_MA, OUT_MB, OUT_D, OUT_K):
        all_left(out)
    left(g_ref.at[:, :, core], out_sems.at[OUT_GC])
    left(gc_ref, out_sems.at[OUT_G])
    for d in XD:
        pl.when(xp(d) < NL)(functools.partial(left, gx_ref.at[d - 1], ky_out_sems.at[NY + d]))
    for d in YD:
        pl.when(yp(d) < NP)(functools.partial(left, ky_ref.at[d - 1], ky_out_sems.at[d]))

    @pl.when(held)
    def _():
        all_left(OUT_KZ)
        all_left(OUT_KY)

    @pl.when(holds_g)
    def _():
        all_left(OUT_GS)
        all_left(OUT_GX)


def exchange(matrix, panel, sizes):
    NX, NY, NZ, TR, WIDTH, PW, NL, LA = sizes
    f32 = jnp.float32
    NP = PW // 2 // NX // 8
    GR = PW // NZ // 2
    LW, LB = PW // NL, PW - LA
    vmem = pl.BlockSpec(memory_space=pltpu.VMEM)
    shape = lambda *s: jax.ShapeDtypeStruct(s, f32)
    V = lambda *s: pltpu.VMEM(s, f32)
    D = lambda n: pltpu.SemaphoreType.DMA((n,))
    return pl.pallas_call(
        functools.partial(comm_kernel, sizes),
        out_shape=[shape(NL, NZ, 2, GR, LW), shape(2, NX, NP, 8, PW), shape(NX, NY, 2, TR, PW),
                   shape(NX, NY, 2, TR, PW), shape(NZ, TR, PW), shape(PW, PW), shape(8, 128)],
        in_specs=[pl.BlockSpec(memory_space=pltpu.HBM)] * 2,
        out_specs=[vmem] * 7,
        scratch_shapes=[
            V(NZ, TR, WIDTH), V(NZ, TR, PW), V(PW, PW), V(160, 8, PW), V(NZ, TR, WIDTH),
            V(NL, NZ, 2, GR, LW), V(NL, GR, LW), V(NL, GR, LW), V(NX - 1, GR, LW), V(GR, LW),
            V(NY - 1, GR, LW),
            V(2, NX, NY, TR, LA), V(2, NY, NX, TR, LB), V(NX, NY, TR, LA), V(NY, NX, TR, LB),
            V(NX - 1, NY, TR, LA), V(NY - 1, TR, LA), V(NY - 1, NX, TR, LB), V(NX, TR, LB),
            V(NX - 1, TR, LB),
            V(NZ, TR, PW), V(NZ - 1, TR, PW), V(2, NX, NP, 8, PW), V(NX, NP, 8, PW),
            V(NX - 1, NP, 8, PW), V(NX, NP, 8, PW), V(NY - 1, 8, PW), V(NZ - 1, 8, PW), V(8, PW),
            D(2), D(12), D(NY + NX), D(NY + 2 * NX), D(NY + 2 * NX), D(NZ - 1), D(NX + NY), D(NX + NY),
            D(NZ - 1), D(NX + NY), D(NZ - 1), D(NX), D(NX + NY), D(NZ - 1), D(NX + NY),
        ],
        compiler_params=pltpu.CompilerParams(
            collective_id=0, has_side_effects=True, vmem_limit_bytes=32 * 2**20),
        name="exchange",
    )(matrix, panel)


def polish(g_ref, n_ref, error):
    blocks, _, _, _, width = g_ref.shape
    size = blocks * width
    gram = jnp.concatenate([g_ref[l].reshape(size, width) for l in range(blocks)], axis=1)
    scaled, eye, s_row, s_col, start = scaled_gram(gram)
    usable = error < 0.25
    guess = n_ref[...] / s_row / s_col

    def step(state):
        count, _, guess = state
        residual = eye - dot_nn(scaled, guess)
        error = jnp.sum(residual * residual)
        return count + 1, error, guess + dot_nn(guess, residual)

    def again(state):
        return jnp.logical_and(state[1] > 1e-8, state[0] < 80)

    state = (0, jnp.where(usable, error, 1.0), jnp.where(usable, guess, start))
    _, _, found = lax.while_loop(again, step, state)
    n_ref[...] = found * s_row * s_col


def finish_kernel(mat_ref, pan_ref, g_ref, k_ref, tc_ref, wc_ref, wr_ref, inv_ref, err_ref, out_ref, n_ref):
    NZ, TR, WIDTH = mat_ref.shape
    PW = pan_ref.shape[2]
    row = lax.axis_index("row")
    z = lax.axis_index("col")
    n_ref[...] = inv_ref[...]
    error = err_ref[0, 0]

    @pl.when(jnp.logical_not(error <= 1e-8))
    def _():
        polish(g_ref, n_ref, error)

    inv = n_ref[...]
    half = k_ref[...]
    proj = half + half.T
    t_rows = pan_ref[...].reshape(NZ * TR, PW)
    w_rows = wr_ref[...].reshape(NZ * TR, PW)
    left = dot_nn(t_rows, inv)
    right = dot_nn(w_rows - 2.0 * dot_nn(left, proj), inv)
    sub = lax.broadcasted_iota(jnp.int32, (TR, WIDTH), 0) + row * TR
    lane = lax.broadcasted_iota(jnp.int32, (TR, WIDTH), 1)
    change = dot_split(left, wc_ref[...], NT) + dot_split(right, tc_ref[...], NT)
    change = change.reshape(NZ, TR, WIDTH)
    for a in range(NZ):
        new = mat_ref[a] - 2.0 * change[a]
        keep = jnp.logical_or(z < a, jnp.logical_and(z == a, sub >= lane))
        out_ref[a] = jnp.where(keep, new, 0.0)


def finish(*operands):
    matrix = operands[0]
    vmem = pl.BlockSpec(memory_space=pltpu.VMEM)
    return pl.pallas_call(
        finish_kernel,
        out_shape=jax.ShapeDtypeStruct(matrix.shape, jnp.float32),
        in_specs=[vmem] * len(operands),
        out_specs=vmem,
        scratch_shapes=[pltpu.VMEM(operands[7].shape, jnp.float32)],
        compiler_params=pltpu.CompilerParams(vmem_limit_bytes=32 * 2**20),
        name="finish",
    )(*operands)


def per_device(matrix, panel):
    NZ, _, TR, WIDTH = matrix.shape
    PW = panel.shape[3]
    NX, NY = PLANES[lax.axis_size("row")]
    lanes = max(PW // 128, 1)
    sizes = (NX, NY, NZ, TR, WIDTH, PW, lanes, PW // lanes if lanes > 1 else PW // 2)
    mat = matrix.reshape(NZ, TR, WIDTH)
    pan = panel.reshape(NZ, TR, PW)
    gram, proj, t_cols, w_cols, w_rows, guess, error = exchange(mat, pan, sizes)
    out = finish(mat, pan, gram, proj.reshape(PW, PW),
                 t_cols.reshape(WIDTH, PW), w_cols.reshape(WIDTH, PW), w_rows, guess, error)
    return out.reshape(NZ, 1, TR, WIDTH)


def solution(mesh):
    in_specs = (P(None, "row", None, "col"), P(None, "row", None, None))
    out_specs = P(None, "row", None, "col")
    return jax.shard_map(
        per_device, mesh=mesh, in_specs=in_specs, out_specs=out_specs, check_vma=False)
```

```python
import functools

import jax
import jax.numpy as jnp
from jax import lax
from jax.experimental import pallas as pl
from jax.experimental.pallas import tpu as pltpu
from jax.sharding import PartitionSpec as P

EXACT = lax.Precision.HIGHEST
PLANES = {64: (4, 8), 8: (2, 2)}


def dot_nn(a, b):
    return lax.dot_general(a, b, (((1,), (0,)), ((), ())), precision=EXACT,
                           preferred_element_type=jnp.float32)


def dot_tn(a, b):
    return lax.dot_general(a, b, (((0,), (0,)), ((), ())), precision=EXACT,
                           preferred_element_type=jnp.float32)


def dot_nt(a, b):
    return lax.dot_general(a, b, (((1,), (1,)), ((), ())), precision=EXACT,
                           preferred_element_type=jnp.float32)


def two_parts(a):
    high = a.astype(jnp.bfloat16)
    return high, (a - high.astype(jnp.float32)).astype(jnp.bfloat16)


def dot_split(a, b, dims):
    ah, al = two_parts(a)
    bh, bl = two_parts(b)
    dot = lambda p, q: lax.dot_general(p, q, (dims, ((), ())), preferred_element_type=jnp.float32)
    return dot(ah, bh) + (dot(ah, bl) + dot(al, bh))


NN, TN, NT = ((1,), (0,)), ((0,), (0,)), ((1,), (1,))


def by_distance(n):
    return sorted(range(1, n), key=lambda d: (min(d, n - d), d))


def scaled_gram(gram):
    n = gram.shape[0]
    eye = jnp.where(lax.broadcasted_iota(jnp.int32, (n, n), 0)
                    == lax.broadcasted_iota(jnp.int32, (n, n), 1), 1.0, 0.0)
    diag = gram * eye
    s_row = lax.rsqrt(jnp.sum(diag, axis=0, keepdims=True))
    s_col = lax.rsqrt(jnp.sum(diag, axis=1, keepdims=True))
    scaled = gram * s_row * s_col
    bound = jnp.max(jnp.sum(jnp.abs(scaled), axis=0, keepdims=True))
    return scaled, eye, s_row, s_col, eye * (2.0 / (1.0 + bound))


COARSE_STEPS = 4
KR = 16


def comm_kernel(sizes, mat_hbm, pan_hbm, g_ref, k_ref, tc_ref, wc_ref, wr_ref, inv_ref, err_ref, left_ref,
                mat_ref, pan_ref, sg_ref, units_ref, h_ref,
                gl_ref, gc_ref, gsum_ref, gx_ref, gsx_ref, gy_ref,
                mpa_ref, mpb_ref, ca_ref, cb_ref, ax_ref, ay_ref, by_ref, bs_ref, bx_ref,
                dp_ref, rz_ref, kp_ref, kc_ref, kx_ref, ks_ref, ky_ref, kz_ref, kf_ref,
                in_sems, out_sems, ky_out_sems, t_sems, w_sems, wz_sems, ma_sems, mb_sems, dz_sems,
                g_sems, gz_sems, ga_sems, k_sems, kz_sems, ka_sems):
    NX, NY, NZ, TR, WIDTH, PW, NL, LA = sizes
    LW = PW // NL
    PAIRS = [(i, j) for i in range(NL) for j in range(i + 1)]
    NP = len(PAIRS) * LW // 2 // NX // KR
    row = lax.axis_index("row")
    z = lax.axis_index("col")
    core = lax.rem(row, 2)
    chip = lax.div(row, 2)
    y = lax.rem(chip, NY)
    x = lax.div(chip, NY)
    other = 1 - core

    def at(x_, y_, c_):
        return (x_ * NY + y_) * 2 + c_

    def xp(d):
        return lax.rem(x + d, NX)

    def yp(d):
        return lax.rem(y + d, NY)

    def zp(d):
        return lax.rem(z + d, NZ)

    to_x = lambda d: (at(xp(d), y, core), z)
    to_y = lambda d: (at(x, yp(d), core), z)
    to_z = lambda d: (row, zp(d))
    to_core = (at(x, y, other), z)

    barrier = pltpu.get_barrier_semaphore()
    peers = ([to_x(d) for d in range(1, NX)] + [to_y(d) for d in range(1, NY)]
             + [to_z(d) for d in range(1, NZ)] + [to_core])
    for peer in peers:
        pl.semaphore_signal(barrier, inc=1, device_id=peer, device_id_type=pl.DeviceIdType.MESH)

    pan_in = pltpu.make_async_copy(pan_hbm, pan_ref, in_sems.at[0])
    mat_in = pltpu.make_async_copy(mat_hbm, mat_ref, in_sems.at[1])
    pan_in.start()
    mat_in.start()

    totals = {}

    def send(src, dst, sem, peer, out):
        words = 1
        for n in src.shape:
            words *= n
        totals[out] = totals.get(out, 0) + words
        pltpu.make_async_remote_copy(
            src_ref=src, dst_ref=dst, send_sem=out_sems.at[out], recv_sem=sem,
            device_id=peer, device_id_type=pl.DeviceIdType.MESH).start()

    def left(ref, sem):
        pltpu.make_async_remote_copy(
            src_ref=ref, dst_ref=ref, send_sem=sem, recv_sem=t_sems.at[0],
            device_id=to_core, device_id_type=pl.DeviceIdType.MESH).wait_send()

    def all_left(out):
        assert totals[out] % (8 * PW) == 0
        left(units_ref.at[pl.ds(0, totals[out] // (8 * PW))], out_sems.at[out])

    def arrive(dst, sem):
        pltpu.make_async_remote_copy(
            src_ref=dst, dst_ref=dst, send_sem=out_sems.at[0], recv_sem=sem,
            device_id=to_core, device_id_type=pl.DeviceIdType.MESH).wait_recv()

    OUT_T, OUT_W, OUT_MA, OUT_MB, OUT_D, OUT_K, OUT_KZ, OUT_KY, OUT_G, OUT_GS, OUT_GX, OUT_GC, OUT_KX = range(13)
    YD, XD, ZD = by_distance(NY), by_distance(NX), by_distance(NZ)

    pan_in.wait()
    tc_ref[x, y, core] = pan_ref[z]
    t_rows = pan_ref[...].reshape(NZ * TR, PW)
    gram = dot_tn(t_rows, t_rows)
    for l in range(NL):
        gl_ref[l] = gram[:, l * LW:(l + 1) * LW].reshape(NZ, 2, PW // NZ // 2, LW)
    mat_in.wait()
    sub = lax.broadcasted_iota(jnp.int32, (TR, WIDTH), 0) + row * TR
    lane = lax.broadcasted_iota(jnp.int32, (TR, WIDTH), 1)
    for a in range(NZ):
        tile = mat_ref[a]
        diag_part = jnp.where(sub > lane, tile, jnp.where(sub == lane, 0.5 * tile, 0.0))
        h_ref[a] = jnp.where(z < a, tile, jnp.where(z == a, diag_part, 0.0))
    XW = WIDTH // NX

    def columns(xb):
        return h_ref[:, :, pl.ds(pl.multiple_of(xb * XW, XW), XW)].reshape(NZ * TR, XW)

    for d in [0] + XD:
        xb = xp(d)
        terms = dot_tn(columns(xb), t_rows).reshape(NY, 2, TR, PW)
        for c in range(2):
            mpa_ref[c, xb] = terms[:, c, :, :LA]
            mpb_ref[c, :, xb] = terms[:, c, :, LA:]
    pl.semaphore_wait(barrier, len(peers))

    own_t = pan_ref.at[z]
    for d in YD:
        send(own_t, tc_ref.at[x, y, core], t_sems.at[d], to_y(d), OUT_T)
    for d in XD:
        send(own_t, tc_ref.at[x, y, core], t_sems.at[NY + d], to_x(d), OUT_T)
    send(gl_ref.at[:, z, other], gc_ref, g_sems.at[0], to_core, OUT_G)
    send(mpb_ref.at[other], cb_ref, mb_sems.at[0], to_core, OUT_MB)
    send(mpa_ref.at[other], ca_ref, ma_sems.at[0], to_core, OUT_MA)

    holds_g = x < NL
    own_l = lax.min(x, NL - 1)
    arrive(gc_ref, g_sems.at[0])
    gsum_ref[...] = gl_ref[:, z, core] + gc_ref[...]
    for d in XD:
        @pl.when(xp(d) < NL)
        def _():
            pltpu.make_async_remote_copy(
                src_ref=gsum_ref.at[lax.min(xp(d), NL - 1)], dst_ref=gx_ref.at[d - 1],
                send_sem=ky_out_sems.at[NY + d], recv_sem=g_sems.at[d],
                device_id=to_x(d), device_id_type=pl.DeviceIdType.MESH).start()

    def forward_t(ds):
        for d in ds:
            tile = tc_ref.at[x, yp(NY - d), core]
            arrive(tile, t_sems.at[d])
            for dx in XD:
                send(tile, tile, t_sems.at[NY + dx], to_x(dx), OUT_T)

    forward_t(YD[:3])

    @pl.when(holds_g)
    def _():
        gs = gsum_ref[own_l]
        for d in XD:
            arrive(gx_ref.at[d - 1], g_sems.at[d])
            gs = gs + gx_ref[d - 1]
        gsx_ref[...] = gs
        for d in YD:
            send(gsx_ref, gy_ref.at[d - 1], g_sems.at[NX + d], to_y(d), OUT_GS)

    arrive(cb_ref, mb_sems.at[0])
    mpb_ref[core] = mpb_ref[core] + cb_ref[...]
    for d in YD:
        send(mpb_ref.at[core, yp(d)], by_ref.at[d - 1], mb_sems.at[d], to_y(d), OUT_MB)

    forward_t(YD[3:])
    send(tc_ref.at[x, :, core], tc_ref.at[x, :, core], t_sems.at[NY + NX], to_core, OUT_T)
    arrive(ca_ref, ma_sems.at[0])
    mpa_ref[core] = mpa_ref[core] + ca_ref[...]

    def project(xb):
        tiles = tc_ref[xb, :, core].reshape(NY * TR, PW)
        return (dot_split(tiles, mpa_ref[core, xb].reshape(NY * TR, LA), TN),
                dot_split(tiles, mpb_ref[core, :, xb].reshape(NY * TR, PW - LA), TN))

    ka, kb = project(x)
    for dx in XD:
        xb = xp(NX - dx)
        arrive(tc_ref.at[xb, :, core], t_sems.at[NY + dx])
        send(tc_ref.at[xb, :, core], tc_ref.at[xb, :, core], t_sems.at[NY + NX + dx], to_core, OUT_T)
        more_a, more_b = project(xb)
        ka, kb = ka + more_a, kb + more_b
        if dx == XD[min(1, len(XD) - 1)]:
            @pl.when(holds_g)
            def _():
                gs = gsx_ref[...]
                for d in YD:
                    arrive(gy_ref.at[d - 1], g_sems.at[NX + d])
                    gs = gs + gy_ref[d - 1]
                g_ref[own_l, z, core] = gs
                own_g = g_ref.at[own_l, z, core]
                for d in ZD:
                    send(own_g, own_g, gz_sems.at[d - 1], to_z(d), OUT_GS)
    terms = jnp.concatenate([ka, kb], axis=1)
    block = lambda i, j: terms[i * LW:(i + 1) * LW, j * LW:(j + 1) * LW]
    lower = [block(i, j) + block(j, i).T for i, j in PAIRS]
    kp_ref[...] = jnp.concatenate(lower, axis=0).reshape(2, NX, NP, KR, LW)
    send(kp_ref.at[other], kc_ref, k_sems.at[0], to_core, OUT_K)

    arrive(tc_ref.at[x, :, other], t_sems.at[NY + NX])
    direct = dot_split(columns(x), tc_ref[x].reshape(XW, PW), NN)

    arrive(kc_ref, k_sems.at[0])
    ks_ref[...] = kp_ref[core] + kc_ref[...]
    for d in XD:
        send(ks_ref.at[xp(d)], kx_ref.at[d - 1], k_sems.at[d], to_x(d), OUT_K)

    for dx in XD:
        xb = xp(NX - dx)
        arrive(tc_ref.at[xb, :, other], t_sems.at[NY + NX + dx])
        direct = direct + dot_split(columns(xb), tc_ref[xb].reshape(XW, PW), NN)
    dp_ref[...] = direct.reshape(NZ, TR, PW)
    for d in ZD:
        send(dp_ref.at[zp(d)], rz_ref.at[d - 1], dz_sems.at[d - 1], to_z(d), OUT_D)

    for d in XD:
        send(mpa_ref.at[core, xp(d)], ax_ref.at[d - 1], ma_sems.at[d], to_x(d), OUT_MA)

    ksum = ks_ref[x]
    for d in XD:
        arrive(kx_ref.at[d - 1], k_sems.at[d])
        ksum = ksum + kx_ref[d - 1]
    ks_ref[x] = ksum
    for d in YD:
        @pl.when(yp(d) < NP)
        def _():
            pltpu.make_async_remote_copy(
                src_ref=ks_ref.at[x, lax.min(yp(d), NP - 1)], dst_ref=ky_ref.at[d - 1],
                send_sem=ky_out_sems.at[d], recv_sem=k_sems.at[NX + d],
                device_id=to_y(d), device_id_type=pl.DeviceIdType.MESH).start()

    part = mpb_ref[core, y]
    for d in YD:
        arrive(by_ref.at[d - 1], mb_sems.at[d])
        part = part + by_ref[d - 1]
    bs_ref[...] = part
    for d in XD:
        send(bs_ref.at[xp(d)], bx_ref.at[d - 1], mb_sems.at[NY + d], to_x(d), OUT_MB)

    part = mpa_ref[core, x]
    for d in XD:
        arrive(ax_ref.at[d - 1], ma_sems.at[d])
        part = part + ax_ref[d - 1]
    mpa_ref[core, x] = part
    for d in YD:
        send(mpa_ref.at[core, x, yp(d)], ay_ref.at[d - 1], ma_sems.at[NX + d], to_y(d), OUT_MA)

    own_g = g_ref.at[own_l, :, core]

    @pl.when(holds_g)
    def _():
        for d in ZD:
            arrive(g_ref.at[own_l, zp(NZ - d), core], gz_sems.at[d - 1])
        for d in XD:
            send(own_g, own_g, ga_sems.at[d], to_x(d), OUT_GX)

    held = y < NP
    yy = lax.min(y, NP - 1)

    @pl.when(held)
    def _():
        ksum = ks_ref[x, yy]
        for d in YD:
            arrive(ky_ref.at[d - 1], k_sems.at[NX + d])
            ksum = ksum + ky_ref[d - 1]
        kf_ref[...] = ksum
        for d in ZD:
            send(kf_ref, kz_ref.at[d - 1], kz_sems.at[d - 1], to_z(d), OUT_KZ)

    part_b = bs_ref[x]
    for d in XD:
        arrive(bx_ref.at[d - 1], mb_sems.at[NY + d])
        part_b = part_b + bx_ref[d - 1]
    part_a = mpa_ref[core, x, y]
    for d in YD:
        arrive(ay_ref.at[d - 1], ma_sems.at[NX + d])
        part_a = part_a + ay_ref[d - 1]
    wsum = dp_ref[z]
    for d in ZD:
        arrive(rz_ref.at[d - 1], dz_sems.at[d - 1])
        wsum = wsum + rz_ref[d - 1]
    wr_ref[z, :, :LA] = wsum[:, :LA] + part_a
    wr_ref[z, :, LA:] = wsum[:, LA:] + part_b
    wc_ref[x, y, core] = wr_ref[z]
    own_w = wc_ref.at[x, y, core]
    for d in YD:
        send(own_w, own_w, w_sems.at[d], to_y(d), OUT_W)
    for d in XD:
        send(own_w, own_w, w_sems.at[NY + d], to_x(d), OUT_W)
    for d in ZD:
        send(wr_ref.at[z], wr_ref.at[z], wz_sems.at[d - 1], to_z(d), OUT_W)

    for d in XD:
        src_l = xp(NX - d)

        @pl.when(src_l < NL)
        def _():
            arrive(g_ref.at[lax.min(src_l, NL - 1), :, core], ga_sems.at[d])
    send(g_ref.at[:, :, core], g_ref.at[:, :, core], ga_sems.at[0], to_core, OUT_GC)

    arrive(g_ref.at[:, :, other], ga_sems.at[0])
    whole = jnp.concatenate([g_ref[l].reshape(PW, LW) for l in range(NL)], axis=1)
    scaled, eye, s_row, s_col, start = scaled_gram(whole)
    sg_ref[...] = scaled
    inv_ref[...] = start

    def newton(dot):
        residual = eye - dot(sg_ref[...], inv_ref[...])
        inv_ref[...] += dot(inv_ref[...], residual)

    coarse = lambda a, b: jnp.dot(a.astype(jnp.bfloat16), b.astype(jnp.bfloat16),
                                  preferred_element_type=jnp.float32)
    fine = lambda a, b: dot_split(a, b, NN)

    for n, d in enumerate(YD):
        tile = wc_ref.at[x, yp(NY - d), core]
        arrive(tile, w_sems.at[d])
        for dx in XD:
            send(tile, tile, w_sems.at[NY + dx], to_x(dx), OUT_W)
        if n < COARSE_STEPS:
            newton(coarse)
    send(wc_ref.at[x, :, core], wc_ref.at[x, :, core], w_sems.at[NY + NX], to_core, OUT_W)
    for _ in range(COARSE_STEPS - len(YD)):
        newton(coarse)

    own_k = k_ref.at[core, x, yy]

    @pl.when(held)
    def _():
        ksum = kf_ref[...]
        for d in ZD:
            arrive(kz_ref.at[d - 1], kz_sems.at[d - 1])
            ksum = ksum + kz_ref[d - 1]
        k_ref[core, x, yy] = ksum
        for d in YD:
            send(own_k, own_k, ka_sems.at[d], to_y(d), OUT_KY)
        for d in XD:
            send(own_k, own_k, ka_sems.at[NY + d], to_x(d), OUT_KX)

    def forward_k(ds):
        for d in ds:
            src_y = yp(NY - d)

            @pl.when(src_y < NP)
            def _():
                piece = k_ref.at[core, x, lax.min(src_y, NP - 1)]
                arrive(piece, ka_sems.at[d])
                for dx in XD:
                    send(piece, piece, ka_sems.at[NY + dx], to_x(dx), OUT_KX)

    def pass_w(dx):
        block = wc_ref.at[xp(NX - dx), :, core]
        arrive(block, w_sems.at[NY + dx])
        send(block, block, w_sems.at[NY + NX + dx], to_core, OUT_W)

    def pass_k(dx):
        block = k_ref.at[core, xp(NX - dx)]
        if dx:
            arrive(block, ka_sems.at[NY + dx])
        send(block, block, ka_sems.at[NY + NX + dx], to_core, OUT_K)

    newton(fine)
    forward_k(YD[:3])
    newton(fine)
    forward_k(YD[3:])
    pass_k(0)
    for dx in XD:
        pass_w(dx)
    newton(fine)
    for dx in XD:
        pass_k(dx)

    residual = eye - dot_nn(sg_ref[...], inv_ref[...])
    err_ref[...] = jnp.full(err_ref.shape, jnp.sum(residual * residual), jnp.float32)
    inv_ref[...] = (inv_ref[...] + fine(inv_ref[...], residual)) * s_row * s_col
    left_ref[...] = dot_nn(pan_ref[...].reshape(NZ * TR, PW), inv_ref[...])

    for d in ZD:
        arrive(wr_ref.at[zp(NZ - d)], wz_sems.at[d - 1])
    arrive(wc_ref.at[x, :, other], w_sems.at[NY + NX])
    for dx in XD:
        arrive(wc_ref.at[xp(NX - dx), :, other], w_sems.at[NY + NX + dx])
    for dx in [0] + XD:
        arrive(k_ref.at[other, xp(NX - dx)], ka_sems.at[NY + NX + dx])
    for out in (OUT_T, OUT_W, OUT_MA, OUT_MB, OUT_D, OUT_K):
        all_left(out)
    left(g_ref.at[:, :, core], out_sems.at[OUT_GC])
    left(kx_ref, out_sems.at[OUT_KX])
    left(gc_ref, out_sems.at[OUT_G])
    for d in XD:
        pl.when(xp(d) < NL)(functools.partial(left, gx_ref.at[d - 1], ky_out_sems.at[NY + d]))
    for d in YD:
        pl.when(yp(d) < NP)(functools.partial(left, ky_ref.at[d - 1], ky_out_sems.at[d]))

    @pl.when(held)
    def _():
        left(kz_ref, out_sems.at[OUT_KZ])
        left(ky_ref, out_sems.at[OUT_KY])

    @pl.when(holds_g)
    def _():
        all_left(OUT_GS)
        all_left(OUT_GX)


def exchange(matrix, panel, sizes):
    NX, NY, NZ, TR, WIDTH, PW, NL, LA = sizes
    f32 = jnp.float32
    GR = PW // NZ // 2
    LW, LB = PW // NL, PW - LA
    NP = NL * (NL + 1) // 2 * LW // 2 // NX // KR
    vmem = pl.BlockSpec(memory_space=pltpu.VMEM)
    shape = lambda *s: jax.ShapeDtypeStruct(s, f32)
    V = lambda *s: pltpu.VMEM(s, f32)
    D = lambda n: pltpu.SemaphoreType.DMA((n,))
    return pl.pallas_call(
        functools.partial(comm_kernel, sizes),
        out_shape=[shape(NL, NZ, 2, GR, LW), shape(2, NX, NP, KR, LW), shape(NX, NY, 2, TR, PW),
                   shape(NX, NY, 2, TR, PW), shape(NZ, TR, PW), shape(PW, PW), shape(8, 128),
                   shape(NZ * TR, PW)],
        in_specs=[pl.BlockSpec(memory_space=pltpu.HBM)] * 2,
        out_specs=[vmem] * 8,
        scratch_shapes=[
            V(NZ, TR, WIDTH), V(NZ, TR, PW), V(PW, PW), V(160, 8, PW), V(NZ, TR, WIDTH),
            V(NL, NZ, 2, GR, LW), V(NL, GR, LW), V(NL, GR, LW), V(NX - 1, GR, LW), V(GR, LW),
            V(NY - 1, GR, LW),
            V(2, NX, NY, TR, LA), V(2, NY, NX, TR, LB), V(NX, NY, TR, LA), V(NY, NX, TR, LB),
            V(NX - 1, NY, TR, LA), V(NY - 1, TR, LA), V(NY - 1, NX, TR, LB), V(NX, TR, LB),
            V(NX - 1, TR, LB),
            V(NZ, TR, PW), V(NZ - 1, TR, PW), V(2, NX, NP, KR, LW), V(NX, NP, KR, LW),
            V(NX - 1, NP, KR, LW), V(NX, NP, KR, LW), V(NY - 1, KR, LW), V(NZ - 1, KR, LW), V(KR, LW),
            D(2), D(13), D(NY + NX), D(NY + 2 * NX), D(NY + 2 * NX), D(NZ - 1), D(NX + NY), D(NX + NY),
            D(NZ - 1), D(NX + NY), D(NZ - 1), D(NX), D(NX + NY), D(NZ - 1), D(2 * NX + NY),
        ],
        compiler_params=pltpu.CompilerParams(
            collective_id=0, has_side_effects=True, vmem_limit_bytes=32 * 2**20),
        name="exchange",
    )(matrix, panel)


def polish(g_ref, n_ref, error):
    blocks, _, _, _, width = g_ref.shape
    size = blocks * width
    gram = jnp.concatenate([g_ref[l].reshape(size, width) for l in range(blocks)], axis=1)
    scaled, eye, s_row, s_col, start = scaled_gram(gram)
    usable = error < 0.25
    guess = n_ref[...] / s_row / s_col

    def step(state):
        count, _, guess = state
        residual = eye - dot_nn(scaled, guess)
        error = jnp.sum(residual * residual)
        return count + 1, error, guess + dot_nn(guess, residual)

    def again(state):
        return jnp.logical_and(state[1] > 1e-8, state[0] < 80)

    state = (0, jnp.where(usable, error, 1.0), jnp.where(usable, guess, start))
    _, _, found = lax.while_loop(again, step, state)
    n_ref[...] = found * s_row * s_col


def finish_kernel(mat_ref, pan_ref, g_ref, k_ref, tc_ref, wc_ref, wr_ref, inv_ref, err_ref, left_ref,
                  out_ref, n_ref, tn_ref):
    NZ, TR, WIDTH = mat_ref.shape
    PW = pan_ref.shape[2]
    row = lax.axis_index("row")
    z = lax.axis_index("col")
    n_ref[...] = inv_ref[...]
    tn_ref[...] = left_ref[...]
    error = err_ref[0, 0]
    t_rows = pan_ref[...].reshape(NZ * TR, PW)

    @pl.when(jnp.logical_not(error <= 1e-8))
    def _():
        polish(g_ref, n_ref, error)
        tn_ref[...] = dot_nn(t_rows, n_ref[...])

    size = k_ref.shape[-1]
    count = PW // size
    lower = k_ref[...].reshape(-1, size)
    block = lambda i, j: lower[(i * (i + 1) // 2 + j) * size:(i * (i + 1) // 2 + j + 1) * size]
    proj = jnp.concatenate([
        jnp.concatenate([block(i, j) if i >= j else block(j, i).T for j in range(count)], axis=1)
        for i in range(count)], axis=0)
    left = tn_ref[...]
    w_rows = wr_ref[...].reshape(NZ * TR, PW)
    right = dot_split(w_rows - 2.0 * dot_split(left, proj, NN), n_ref[...], NN)
    sub = lax.broadcasted_iota(jnp.int32, (TR, WIDTH), 0) + row * TR
    lane = lax.broadcasted_iota(jnp.int32, (TR, WIDTH), 1)
    change = dot_split(left, wc_ref[...], NT) + dot_split(right, tc_ref[...], NT)
    change = change.reshape(NZ, TR, WIDTH)
    for a in range(NZ):
        new = mat_ref[a] - 2.0 * change[a]
        keep = jnp.logical_or(z < a, jnp.logical_and(z == a, sub >= lane))
        out_ref[a] = jnp.where(keep, new, 0.0)


def finish(*operands):
    matrix = operands[0]
    vmem = pl.BlockSpec(memory_space=pltpu.VMEM)
    return pl.pallas_call(
        finish_kernel,
        out_shape=jax.ShapeDtypeStruct(matrix.shape, jnp.float32),
        in_specs=[vmem] * len(operands),
        out_specs=vmem,
        scratch_shapes=[pltpu.VMEM(operands[7].shape, jnp.float32), pltpu.VMEM(operands[9].shape, jnp.float32)],
        compiler_params=pltpu.CompilerParams(vmem_limit_bytes=32 * 2**20),
        name="finish",
    )(*operands)


def per_device(matrix, panel):
    NZ, _, TR, WIDTH = matrix.shape
    PW = panel.shape[3]
    NX, NY = PLANES[lax.axis_size("row")]
    lanes = max(PW // 128, 1)
    sizes = (NX, NY, NZ, TR, WIDTH, PW, lanes, PW // lanes if lanes > 1 else PW // 2)
    mat = matrix.reshape(NZ, TR, WIDTH)
    pan = panel.reshape(NZ, TR, PW)
    gram, proj, t_cols, w_cols, w_rows, guess, error, left = exchange(mat, pan, sizes)
    out = finish(mat, pan, gram, proj,
                 t_cols.reshape(WIDTH, PW), w_cols.reshape(WIDTH, PW), w_rows, guess, error, left)
    return out.reshape(NZ, 1, TR, WIDTH)


def solution(mesh):
    in_specs = (P(None, "row", None, "col"), P(None, "row", None, None))
    out_specs = P(None, "row", None, "col")
    return jax.shard_map(
        per_device, mesh=mesh, in_specs=in_specs, out_specs=out_specs, check_vma=False)
```

```python
import functools

import jax
import jax.numpy as jnp
from jax import lax
from jax.experimental import pallas as pl
from jax.experimental.pallas import tpu as pltpu
from jax.sharding import PartitionSpec as P

EXACT = lax.Precision.HIGHEST
PLANES = {64: (4, 8), 8: (2, 2)}


def dot_nn(a, b):
    return lax.dot_general(a, b, (((1,), (0,)), ((), ())), precision=EXACT,
                           preferred_element_type=jnp.float32)


def dot_tn(a, b):
    return lax.dot_general(a, b, (((0,), (0,)), ((), ())), precision=EXACT,
                           preferred_element_type=jnp.float32)


def dot_nt(a, b):
    return lax.dot_general(a, b, (((1,), (1,)), ((), ())), precision=EXACT,
                           preferred_element_type=jnp.float32)


def two_parts(a):
    high = a.astype(jnp.bfloat16)
    return high, (a - high.astype(jnp.float32)).astype(jnp.bfloat16)


def dot_split(a, b, dims):
    ah, al = two_parts(a)
    bh, bl = two_parts(b)
    dot = lambda p, q: lax.dot_general(p, q, (dims, ((), ())), preferred_element_type=jnp.float32)
    return dot(ah, bh) + (dot(ah, bl) + dot(al, bh))


NN, TN, NT = ((1,), (0,)), ((0,), (0,)), ((1,), (1,))


def by_distance(n):
    return sorted(range(1, n), key=lambda d: (min(d, n - d), d))


def scaled_gram(gram):
    n = gram.shape[0]
    eye = jnp.where(lax.broadcasted_iota(jnp.int32, (n, n), 0)
                    == lax.broadcasted_iota(jnp.int32, (n, n), 1), 1.0, 0.0)
    diag = gram * eye
    s_row = lax.rsqrt(jnp.sum(diag, axis=0, keepdims=True))
    s_col = lax.rsqrt(jnp.sum(diag, axis=1, keepdims=True))
    scaled = gram * s_row * s_col
    bound = jnp.max(jnp.sum(jnp.abs(scaled), axis=0, keepdims=True))
    return scaled, eye, s_row, s_col, eye * (2.0 / (1.0 + bound))


COARSE_STEPS = 5
SMALL = 1e-6
KR = 16


def comm_kernel(sizes, mat_ref, pan_ref, g_ref, k_ref, tc_ref, wc_ref, wr_ref, inv_ref, err_ref, left_ref,
                sg_ref, units_ref, h_ref,
                gl_ref, gc_ref, gsum_ref, gx_ref, gsx_ref, gy_ref,
                mpa_ref, mpb_ref, ca_ref, cb_ref, ax_ref, ay_ref, by_ref, bs_ref, bx_ref,
                dp_ref, rz_ref, kp_ref, kc_ref, kx_ref, ks_ref, ky_ref, kz_ref, kf_ref,
                out_sems, ky_out_sems, t_sems, w_sems, wz_sems, ma_sems, mb_sems, dz_sems,
                g_sems, gz_sems, ga_sems, k_sems, kz_sems, ka_sems):
    NX, NY, NZ, TR, WIDTH, PW, NL, LA = sizes
    LW = PW // NL
    PAIRS = [(i, j) for i in range(NL) for j in range(i + 1)]
    NP = len(PAIRS) * LW // 2 // NX // KR
    row = lax.axis_index("row")
    z = lax.axis_index("col")
    core = lax.rem(row, 2)
    chip = lax.div(row, 2)
    y = lax.rem(chip, NY)
    x = lax.div(chip, NY)
    other = 1 - core

    def at(x_, y_, c_):
        return (x_ * NY + y_) * 2 + c_

    def xp(d):
        return lax.rem(x + d, NX)

    def yp(d):
        return lax.rem(y + d, NY)

    def zp(d):
        return lax.rem(z + d, NZ)

    to_x = lambda d: (at(xp(d), y, core), z)
    to_y = lambda d: (at(x, yp(d), core), z)
    to_z = lambda d: (row, zp(d))
    to_core = (at(x, y, other), z)

    barrier = pltpu.get_barrier_semaphore()
    peers = ([to_x(d) for d in range(1, NX)] + [to_y(d) for d in range(1, NY)]
             + [to_z(d) for d in range(1, NZ)] + [to_core])
    for peer in peers:
        pl.semaphore_signal(barrier, inc=1, device_id=peer, device_id_type=pl.DeviceIdType.MESH)

    totals = {}

    def send(src, dst, sem, peer, out):
        words = 1
        for n in src.shape:
            words *= n
        totals[out] = totals.get(out, 0) + words
        pltpu.make_async_remote_copy(
            src_ref=src, dst_ref=dst, send_sem=out_sems.at[out], recv_sem=sem,
            device_id=peer, device_id_type=pl.DeviceIdType.MESH).start()

    def left(ref, sem):
        pltpu.make_async_remote_copy(
            src_ref=ref, dst_ref=ref, send_sem=sem, recv_sem=t_sems.at[0],
            device_id=to_core, device_id_type=pl.DeviceIdType.MESH).wait_send()

    def all_left(out):
        assert totals[out] % (8 * PW) == 0
        left(units_ref.at[pl.ds(0, totals[out] // (8 * PW))], out_sems.at[out])

    def arrive(dst, sem):
        pltpu.make_async_remote_copy(
            src_ref=dst, dst_ref=dst, send_sem=out_sems.at[0], recv_sem=sem,
            device_id=to_core, device_id_type=pl.DeviceIdType.MESH).wait_recv()

    OUT_T, OUT_W, OUT_MA, OUT_MB, OUT_D, OUT_K, OUT_KZ, OUT_KY, OUT_G, OUT_GS, OUT_GX, OUT_GC, OUT_KX = range(13)
    YD, XD, ZD = by_distance(NY), by_distance(NX), by_distance(NZ)

    sub = lax.broadcasted_iota(jnp.int32, (TR, WIDTH), 0) + row * TR
    lane = lax.broadcasted_iota(jnp.int32, (TR, WIDTH), 1)
    for a in range(NZ):
        tile = mat_ref[a]
        diag_part = jnp.where(sub > lane, tile, jnp.where(sub == lane, 0.5 * tile, 0.0))
        h_ref[a] = jnp.where(z < a, tile, jnp.where(z == a, diag_part, 0.0))
    pl.semaphore_wait(barrier, len(peers))

    own_t = pan_ref.at[z]
    for d in YD:
        send(own_t, tc_ref.at[x, y, core], t_sems.at[d], to_y(d), OUT_T)
    for d in XD:
        send(own_t, tc_ref.at[x, y, core], t_sems.at[NY + d], to_x(d), OUT_T)
    tc_ref[x, y, core] = pan_ref[z]

    t_rows = pan_ref[...].reshape(NZ * TR, PW)
    gram = dot_tn(t_rows, t_rows)
    for l in range(NL):
        gl_ref[l] = gram[:, l * LW:(l + 1) * LW].reshape(NZ, 2, PW // NZ // 2, LW)
    send(gl_ref.at[:, z, other], gc_ref, g_sems.at[0], to_core, OUT_G)
    XW = WIDTH // NX

    def columns(xb):
        return h_ref[:, :, pl.ds(pl.multiple_of(xb * XW, XW), XW)].reshape(NZ * TR, XW)

    for d in [0] + XD:
        xb = xp(d)
        terms = dot_split(columns(xb), t_rows, TN).reshape(NY, 2, TR, PW)
        for c in range(2):
            mpa_ref[c, xb] = terms[:, c, :, :LA]
            mpb_ref[c, :, xb] = terms[:, c, :, LA:]
    send(mpb_ref.at[other], cb_ref, mb_sems.at[0], to_core, OUT_MB)
    send(mpa_ref.at[other], ca_ref, ma_sems.at[0], to_core, OUT_MA)

    holds_g = x < NL
    own_l = lax.min(x, NL - 1)
    arrive(gc_ref, g_sems.at[0])
    gsum_ref[...] = gl_ref[:, z, core] + gc_ref[...]
    for d in XD:
        @pl.when(xp(d) < NL)
        def _():
            pltpu.make_async_remote_copy(
                src_ref=gsum_ref.at[lax.min(xp(d), NL - 1)], dst_ref=gx_ref.at[d - 1],
                send_sem=ky_out_sems.at[NY + d], recv_sem=g_sems.at[d],
                device_id=to_x(d), device_id_type=pl.DeviceIdType.MESH).start()

    def forward_t(ds):
        for d in ds:
            tile = tc_ref.at[x, yp(NY - d), core]
            arrive(tile, t_sems.at[d])
            for dx in XD:
                send(tile, tile, t_sems.at[NY + dx], to_x(dx), OUT_T)

    forward_t(YD[:3])

    @pl.when(holds_g)
    def _():
        gs = gsum_ref[own_l]
        for d in XD:
            arrive(gx_ref.at[d - 1], g_sems.at[d])
            gs = gs + gx_ref[d - 1]
        gsx_ref[...] = gs
        for d in YD:
            send(gsx_ref, gy_ref.at[d - 1], g_sems.at[NX + d], to_y(d), OUT_GS)

    arrive(cb_ref, mb_sems.at[0])
    mpb_ref[core] = mpb_ref[core] + cb_ref[...]
    for d in YD:
        send(mpb_ref.at[core, yp(d)], by_ref.at[d - 1], mb_sems.at[d], to_y(d), OUT_MB)

    forward_t(YD[3:])
    send(tc_ref.at[x, :, core], tc_ref.at[x, :, core], t_sems.at[NY + NX], to_core, OUT_T)
    arrive(ca_ref, ma_sems.at[0])
    mpa_ref[core] = mpa_ref[core] + ca_ref[...]

    def project(xb):
        tiles = tc_ref[xb, :, core].reshape(NY * TR, PW)
        return (dot_split(tiles, mpa_ref[core, xb].reshape(NY * TR, LA), TN),
                dot_split(tiles, mpb_ref[core, :, xb].reshape(NY * TR, PW - LA), TN))

    ka, kb = project(x)
    for dx in XD:
        xb = xp(NX - dx)
        arrive(tc_ref.at[xb, :, core], t_sems.at[NY + dx])
        send(tc_ref.at[xb, :, core], tc_ref.at[xb, :, core], t_sems.at[NY + NX + dx], to_core, OUT_T)
        more_a, more_b = project(xb)
        ka, kb = ka + more_a, kb + more_b
        if dx == XD[min(1, len(XD) - 1)]:
            @pl.when(holds_g)
            def _():
                gs = gsx_ref[...]
                for d in YD:
                    arrive(gy_ref.at[d - 1], g_sems.at[NX + d])
                    gs = gs + gy_ref[d - 1]
                g_ref[own_l, z, core] = gs
                own_g = g_ref.at[own_l, z, core]
                for d in ZD:
                    send(own_g, own_g, gz_sems.at[d - 1], to_z(d), OUT_GS)
    terms = jnp.concatenate([ka, kb], axis=1)
    block = lambda i, j: terms[i * LW:(i + 1) * LW, j * LW:(j + 1) * LW]
    lower = [block(i, j) + block(j, i).T for i, j in PAIRS]
    kp_ref[...] = jnp.concatenate(lower, axis=0).reshape(2, NX, NP, KR, LW)
    send(kp_ref.at[other], kc_ref, k_sems.at[0], to_core, OUT_K)

    arrive(tc_ref.at[x, :, other], t_sems.at[NY + NX])
    direct = dot_split(columns(x), tc_ref[x].reshape(XW, PW), NN)

    arrive(kc_ref, k_sems.at[0])
    ks_ref[...] = kp_ref[core] + kc_ref[...]
    for d in XD:
        send(ks_ref.at[xp(d)], kx_ref.at[d - 1], k_sems.at[d], to_x(d), OUT_K)

    for dx in XD:
        xb = xp(NX - dx)
        arrive(tc_ref.at[xb, :, other], t_sems.at[NY + NX + dx])
        direct = direct + dot_split(columns(xb), tc_ref[xb].reshape(XW, PW), NN)
    dp_ref[...] = direct.reshape(NZ, TR, PW)
    for d in ZD:
        send(dp_ref.at[zp(d)], rz_ref.at[d - 1], dz_sems.at[d - 1], to_z(d), OUT_D)

    for d in XD:
        send(mpa_ref.at[core, xp(d)], ax_ref.at[d - 1], ma_sems.at[d], to_x(d), OUT_MA)

    ksum = ks_ref[x]
    for d in XD:
        arrive(kx_ref.at[d - 1], k_sems.at[d])
        ksum = ksum + kx_ref[d - 1]
    ks_ref[x] = ksum
    for d in YD:
        @pl.when(yp(d) < NP)
        def _():
            pltpu.make_async_remote_copy(
                src_ref=ks_ref.at[x, lax.min(yp(d), NP - 1)], dst_ref=ky_ref.at[d - 1],
                send_sem=ky_out_sems.at[d], recv_sem=k_sems.at[NX + d],
                device_id=to_y(d), device_id_type=pl.DeviceIdType.MESH).start()

    part = mpb_ref[core, y]
    for d in YD:
        arrive(by_ref.at[d - 1], mb_sems.at[d])
        part = part + by_ref[d - 1]
    bs_ref[...] = part
    for d in XD:
        send(bs_ref.at[xp(d)], bx_ref.at[d - 1], mb_sems.at[NY + d], to_x(d), OUT_MB)

    part = mpa_ref[core, x]
    for d in XD:
        arrive(ax_ref.at[d - 1], ma_sems.at[d])
        part = part + ax_ref[d - 1]
    mpa_ref[core, x] = part
    for d in YD:
        send(mpa_ref.at[core, x, yp(d)], ay_ref.at[d - 1], ma_sems.at[NX + d], to_y(d), OUT_MA)

    own_g = g_ref.at[own_l, :, core]

    @pl.when(holds_g)
    def _():
        for d in ZD:
            arrive(g_ref.at[own_l, zp(NZ - d), core], gz_sems.at[d - 1])
        for d in XD:
            send(own_g, own_g, ga_sems.at[d], to_x(d), OUT_GX)

    held = y < NP
    yy = lax.min(y, NP - 1)

    @pl.when(held)
    def _():
        ksum = ks_ref[x, yy]
        for d in YD:
            arrive(ky_ref.at[d - 1], k_sems.at[NX + d])
            ksum = ksum + ky_ref[d - 1]
        kf_ref[...] = ksum
        for d in ZD:
            send(kf_ref, kz_ref.at[d - 1], kz_sems.at[d - 1], to_z(d), OUT_KZ)

    part_b = bs_ref[x]
    for d in XD:
        arrive(bx_ref.at[d - 1], mb_sems.at[NY + d])
        part_b = part_b + bx_ref[d - 1]
    part_a = mpa_ref[core, x, y]
    for d in YD:
        arrive(ay_ref.at[d - 1], ma_sems.at[NX + d])
        part_a = part_a + ay_ref[d - 1]
    wsum = dp_ref[z]
    for d in ZD:
        arrive(rz_ref.at[d - 1], dz_sems.at[d - 1])
        wsum = wsum + rz_ref[d - 1]
    wr_ref[z, :, :LA] = wsum[:, :LA] + part_a
    wr_ref[z, :, LA:] = wsum[:, LA:] + part_b
    wc_ref[x, y, core] = wr_ref[z]
    own_w = wc_ref.at[x, y, core]
    for d in YD:
        send(own_w, own_w, w_sems.at[d], to_y(d), OUT_W)
    for d in XD:
        send(own_w, own_w, w_sems.at[NY + d], to_x(d), OUT_W)
    for d in ZD:
        send(wr_ref.at[z], wr_ref.at[z], wz_sems.at[d - 1], to_z(d), OUT_W)

    for d in XD:
        src_l = xp(NX - d)

        @pl.when(src_l < NL)
        def _():
            arrive(g_ref.at[lax.min(src_l, NL - 1), :, core], ga_sems.at[d])
    send(g_ref.at[:, :, core], g_ref.at[:, :, core], ga_sems.at[0], to_core, OUT_GC)

    own_k = k_ref.at[core, x, yy]

    @pl.when(held)
    def _():
        ksum = kf_ref[...]
        for d in ZD:
            arrive(kz_ref.at[d - 1], kz_sems.at[d - 1])
            ksum = ksum + kz_ref[d - 1]
        k_ref[core, x, yy] = ksum
        for d in YD:
            send(own_k, own_k, ka_sems.at[d], to_y(d), OUT_KY)
        for d in XD:
            send(own_k, own_k, ka_sems.at[NY + d], to_x(d), OUT_KX)

    arrive(g_ref.at[:, :, other], ga_sems.at[0])
    whole = jnp.concatenate([g_ref[l].reshape(PW, LW) for l in range(NL)], axis=1)
    scaled, eye, s_row, s_col, start = scaled_gram(whole)
    sg_ref[...] = scaled
    inv_ref[...] = start

    def newton(dot):
        residual = eye - dot(sg_ref[...], inv_ref[...])
        inv_ref[...] += dot(inv_ref[...], residual)

    coarse = lambda a, b: jnp.dot(a.astype(jnp.bfloat16), b.astype(jnp.bfloat16),
                                  preferred_element_type=jnp.float32)
    fine = lambda a, b: dot_split(a, b, NN)

    for n, d in enumerate(YD):
        tile = wc_ref.at[x, yp(NY - d), core]
        arrive(tile, w_sems.at[d])
        for dx in XD:
            send(tile, tile, w_sems.at[NY + dx], to_x(dx), OUT_W)
        if n < COARSE_STEPS:
            newton(coarse)
    send(wc_ref.at[x, :, core], wc_ref.at[x, :, core], w_sems.at[NY + NX], to_core, OUT_W)
    for _ in range(COARSE_STEPS - len(YD)):
        newton(coarse)

    def forward_k(ds):
        for d in ds:
            src_y = yp(NY - d)

            @pl.when(src_y < NP)
            def _():
                piece = k_ref.at[core, x, lax.min(src_y, NP - 1)]
                arrive(piece, ka_sems.at[d])
                for dx in XD:
                    send(piece, piece, ka_sems.at[NY + dx], to_x(dx), OUT_KX)

    def pass_w(dx):
        block = wc_ref.at[xp(NX - dx), :, core]
        arrive(block, w_sems.at[NY + dx])
        send(block, block, w_sems.at[NY + NX + dx], to_core, OUT_W)

    def pass_k(dx):
        block = k_ref.at[core, xp(NX - dx)]
        if dx:
            arrive(block, ka_sems.at[NY + dx])
        send(block, block, ka_sems.at[NY + NX + dx], to_core, OUT_K)

    forward_k(YD[:3])
    newton(fine)
    forward_k(YD[3:])
    pass_k(0)
    residual = eye - dot_nn(sg_ref[...], inv_ref[...])
    err_ref[...] = jnp.full(err_ref.shape, jnp.sum(residual * residual), jnp.float32)
    inv_ref[...] = (inv_ref[...] + fine(inv_ref[...], residual)) * s_row * s_col
    for dx in XD:
        pass_w(dx)
    for dx in XD:
        pass_k(dx)
    left_ref[...] = dot_nn(pan_ref[...].reshape(NZ * TR, PW), inv_ref[...])

    for d in ZD:
        arrive(wr_ref.at[zp(NZ - d)], wz_sems.at[d - 1])
    arrive(wc_ref.at[x, :, other], w_sems.at[NY + NX])
    for dx in XD:
        arrive(wc_ref.at[xp(NX - dx), :, other], w_sems.at[NY + NX + dx])
    for dx in [0] + XD:
        arrive(k_ref.at[other, xp(NX - dx)], ka_sems.at[NY + NX + dx])
    for out in (OUT_T, OUT_W, OUT_MA, OUT_MB, OUT_D, OUT_K):
        all_left(out)
    left(g_ref.at[:, :, core], out_sems.at[OUT_GC])
    left(kx_ref, out_sems.at[OUT_KX])
    left(gc_ref, out_sems.at[OUT_G])
    for d in XD:
        pl.when(xp(d) < NL)(functools.partial(left, gx_ref.at[d - 1], ky_out_sems.at[NY + d]))
    for d in YD:
        pl.when(yp(d) < NP)(functools.partial(left, ky_ref.at[d - 1], ky_out_sems.at[d]))

    @pl.when(held)
    def _():
        left(kz_ref, out_sems.at[OUT_KZ])
        left(ky_ref, out_sems.at[OUT_KY])

    @pl.when(holds_g)
    def _():
        all_left(OUT_GS)
        all_left(OUT_GX)


def exchange(matrix, panel, sizes):
    NX, NY, NZ, TR, WIDTH, PW, NL, LA = sizes
    f32 = jnp.float32
    GR = PW // NZ // 2
    LW, LB = PW // NL, PW - LA
    NP = NL * (NL + 1) // 2 * LW // 2 // NX // KR
    vmem = pl.BlockSpec(memory_space=pltpu.VMEM)
    shape = lambda *s: jax.ShapeDtypeStruct(s, f32)
    V = lambda *s: pltpu.VMEM(s, f32)
    D = lambda n: pltpu.SemaphoreType.DMA((n,))
    return pl.pallas_call(
        functools.partial(comm_kernel, sizes),
        out_shape=[shape(NL, NZ, 2, GR, LW), shape(2, NX, NP, KR, LW), shape(NX, NY, 2, TR, PW),
                   shape(NX, NY, 2, TR, PW), shape(NZ, TR, PW), shape(PW, PW), shape(8, 128),
                   shape(NZ * TR, PW)],
        in_specs=[vmem] * 2,
        out_specs=[vmem] * 8,
        scratch_shapes=[
            V(PW, PW), V(160, 8, PW), V(NZ, TR, WIDTH),
            V(NL, NZ, 2, GR, LW), V(NL, GR, LW), V(NL, GR, LW), V(NX - 1, GR, LW), V(GR, LW),
            V(NY - 1, GR, LW),
            V(2, NX, NY, TR, LA), V(2, NY, NX, TR, LB), V(NX, NY, TR, LA), V(NY, NX, TR, LB),
            V(NX - 1, NY, TR, LA), V(NY - 1, TR, LA), V(NY - 1, NX, TR, LB), V(NX, TR, LB),
            V(NX - 1, TR, LB),
            V(NZ, TR, PW), V(NZ - 1, TR, PW), V(2, NX, NP, KR, LW), V(NX, NP, KR, LW),
            V(NX - 1, NP, KR, LW), V(NX, NP, KR, LW), V(NY - 1, KR, LW), V(NZ - 1, KR, LW), V(KR, LW),
            D(13), D(NY + NX), D(NY + 2 * NX), D(NY + 2 * NX), D(NZ - 1), D(NX + NY), D(NX + NY),
            D(NZ - 1), D(NX + NY), D(NZ - 1), D(NX), D(NX + NY), D(NZ - 1), D(2 * NX + NY),
        ],
        compiler_params=pltpu.CompilerParams(
            collective_id=0, has_side_effects=True, vmem_limit_bytes=32 * 2**20),
        name="exchange",
    )(matrix, panel)


def polish(g_ref, n_ref, error):
    blocks, _, _, _, width = g_ref.shape
    size = blocks * width
    gram = jnp.concatenate([g_ref[l].reshape(size, width) for l in range(blocks)], axis=1)
    scaled, eye, s_row, s_col, start = scaled_gram(gram)
    usable = error < 0.25
    guess = n_ref[...] / s_row / s_col

    def step(state):
        count, _, guess = state
        residual = eye - dot_nn(scaled, guess)
        error = jnp.sum(residual * residual)
        return count + 1, error, guess + dot_nn(guess, residual)

    def again(state):
        return jnp.logical_and(state[1] > SMALL, state[0] < 80)

    state = (0, jnp.where(usable, error, 1.0), jnp.where(usable, guess, start))
    _, _, found = lax.while_loop(again, step, state)
    n_ref[...] = found * s_row * s_col


def finish_kernel(mat_ref, pan_ref, g_ref, k_ref, tc_ref, wc_ref, wr_ref, inv_ref, err_ref, left_ref,
                  out_ref, n_ref, tn_ref):
    NZ, TR, WIDTH = mat_ref.shape
    PW = pan_ref.shape[2]
    row = lax.axis_index("row")
    z = lax.axis_index("col")
    n_ref[...] = inv_ref[...]
    tn_ref[...] = left_ref[...]
    error = err_ref[0, 0]
    t_rows = pan_ref[...].reshape(NZ * TR, PW)

    @pl.when(jnp.logical_not(error <= SMALL))
    def _():
        polish(g_ref, n_ref, error)
        tn_ref[...] = dot_nn(t_rows, n_ref[...])

    size = k_ref.shape[-1]
    count = PW // size
    lower = k_ref[...].reshape(-1, size)
    block = lambda i, j: lower[(i * (i + 1) // 2 + j) * size:(i * (i + 1) // 2 + j + 1) * size]
    proj = jnp.concatenate([
        jnp.concatenate([block(i, j) if i >= j else block(j, i).T for j in range(count)], axis=1)
        for i in range(count)], axis=0)
    left = tn_ref[...]
    w_rows = wr_ref[...].reshape(NZ * TR, PW)
    right = dot_split(w_rows - 2.0 * dot_split(left, proj, NN), n_ref[...], NN)
    sub = lax.broadcasted_iota(jnp.int32, (TR, WIDTH), 0) + row * TR
    lane = lax.broadcasted_iota(jnp.int32, (TR, WIDTH), 1)
    change = dot_split(left, wc_ref[...], NT) + dot_split(right, tc_ref[...], NT)
    change = change.reshape(NZ, TR, WIDTH)
    for a in range(NZ):
        new = mat_ref[a] - 2.0 * change[a]
        keep = jnp.logical_or(z < a, jnp.logical_and(z == a, sub >= lane))
        out_ref[a] = jnp.where(keep, new, 0.0)


def finish(*operands):
    matrix = operands[0]
    vmem = pl.BlockSpec(memory_space=pltpu.VMEM)
    return pl.pallas_call(
        finish_kernel,
        out_shape=jax.ShapeDtypeStruct(matrix.shape, jnp.float32),
        in_specs=[vmem] * len(operands),
        out_specs=vmem,
        scratch_shapes=[pltpu.VMEM(operands[7].shape, jnp.float32), pltpu.VMEM(operands[9].shape, jnp.float32)],
        compiler_params=pltpu.CompilerParams(vmem_limit_bytes=32 * 2**20),
        name="finish",
    )(*operands)


def per_device(matrix, panel):
    NZ, _, TR, WIDTH = matrix.shape
    PW = panel.shape[3]
    NX, NY = PLANES[lax.axis_size("row")]
    lanes = max(PW // 128, 1)
    sizes = (NX, NY, NZ, TR, WIDTH, PW, lanes, PW // lanes if lanes > 1 else PW // 2)
    mat = matrix.reshape(NZ, TR, WIDTH)
    pan = panel.reshape(NZ, TR, PW)
    gram, proj, t_cols, w_cols, w_rows, guess, error, left = exchange(mat, pan, sizes)
    out = finish(mat, pan, gram, proj,
                 t_cols.reshape(WIDTH, PW), w_cols.reshape(WIDTH, PW), w_rows, guess, error, left)
    return out.reshape(NZ, 1, TR, WIDTH)


def solution(mesh):
    in_specs = (P(None, "row", None, "col"), P(None, "row", None, None))
    out_specs = P(None, "row", None, "col")
    return jax.shard_map(
        per_device, mesh=mesh, in_specs=in_specs, out_specs=out_specs, check_vma=False)
```

```python
import functools

import jax
import jax.numpy as jnp
from jax import lax
from jax.experimental import pallas as pl
from jax.experimental.pallas import tpu as pltpu
from jax.sharding import PartitionSpec as P

EXACT = lax.Precision.HIGHEST
PLANES = {64: (4, 8), 8: (2, 2)}


def dot_nn(a, b):
    return lax.dot_general(a, b, (((1,), (0,)), ((), ())), precision=EXACT,
                           preferred_element_type=jnp.float32)


def dot_tn(a, b):
    return lax.dot_general(a, b, (((0,), (0,)), ((), ())), precision=EXACT,
                           preferred_element_type=jnp.float32)


def dot_nt(a, b):
    return lax.dot_general(a, b, (((1,), (1,)), ((), ())), precision=EXACT,
                           preferred_element_type=jnp.float32)


def two_parts(a):
    high = a.astype(jnp.bfloat16)
    return high, (a - high.astype(jnp.float32)).astype(jnp.bfloat16)


def dot_split(a, b, dims):
    ah, al = two_parts(a)
    bh, bl = two_parts(b)
    dot = lambda p, q: lax.dot_general(p, q, (dims, ((), ())), preferred_element_type=jnp.float32)
    return dot(ah, bh) + (dot(ah, bl) + dot(al, bh))


NN, TN, NT = ((1,), (0,)), ((0,), (0,)), ((1,), (1,))


def by_distance(n):
    return sorted(range(1, n), key=lambda d: (min(d, n - d), d))


def scaled_gram(gram):
    n = gram.shape[0]
    eye = jnp.where(lax.broadcasted_iota(jnp.int32, (n, n), 0)
                    == lax.broadcasted_iota(jnp.int32, (n, n), 1), 1.0, 0.0)
    diag = gram * eye
    s_row = lax.rsqrt(jnp.sum(diag, axis=0, keepdims=True))
    s_col = lax.rsqrt(jnp.sum(diag, axis=1, keepdims=True))
    scaled = gram * s_row * s_col
    bound = jnp.max(jnp.sum(jnp.abs(scaled), axis=0, keepdims=True))
    return scaled, eye, s_row, s_col, eye * (2.0 / (1.0 + bound))


COARSE_STEPS = 5
SMALL = 1e-6
KR = 16


def comm_kernel(sizes, mat_ref, pan_ref, g_ref, k_ref, tc_ref, wc_ref, wr_ref, inv_ref, err_ref, left_ref,
                sg_ref, units_ref, h_ref,
                gl_ref, gc_ref, gsum_ref, gx_ref, gsx_ref, gy_ref,
                mpa_ref, mpb_ref, ca_ref, cb_ref, ax_ref, ay_ref, by_ref, bs_ref, bx_ref,
                dp_ref, rz_ref, kp_ref, kc_ref, kx_ref, ks_ref, ky_ref, kz_ref, kf_ref,
                out_sems, ky_out_sems, t_sems, w_sems, wz_sems, ma_sems, mb_sems, dz_sems,
                g_sems, gz_sems, ga_sems, k_sems, kz_sems, ka_sems):
    NX, NY, NZ, TR, WIDTH, PW, NL, LA = sizes
    LW = PW // NL
    PAIRS = [(i, j) for i in range(NL) for j in range(i + 1)]
    NP = len(PAIRS) * LW // 2 // NX // KR
    row = lax.axis_index("row")
    z = lax.axis_index("col")
    core = lax.rem(row, 2)
    chip = lax.div(row, 2)
    y = lax.rem(chip, NY)
    x = lax.div(chip, NY)
    other = 1 - core

    def at(x_, y_, c_):
        return (x_ * NY + y_) * 2 + c_

    def xp(d):
        return lax.rem(x + d, NX)

    def yp(d):
        return lax.rem(y + d, NY)

    def zp(d):
        return lax.rem(z + d, NZ)

    to_x = lambda d: (at(xp(d), y, core), z)
    to_y = lambda d: (at(x, yp(d), core), z)
    to_z = lambda d: (row, zp(d))
    to_core = (at(x, y, other), z)

    barrier = pltpu.get_barrier_semaphore()
    peers = ([to_x(d) for d in range(1, NX)] + [to_y(d) for d in range(1, NY)]
             + [to_z(d) for d in range(1, NZ)] + [to_core])
    for peer in peers:
        pl.semaphore_signal(barrier, inc=1, device_id=peer, device_id_type=pl.DeviceIdType.MESH)

    totals = {}

    def send(src, dst, sem, peer, out):
        words = 1
        for n in src.shape:
            words *= n
        totals[out] = totals.get(out, 0) + words
        pltpu.make_async_remote_copy(
            src_ref=src, dst_ref=dst, send_sem=out_sems.at[out], recv_sem=sem,
            device_id=peer, device_id_type=pl.DeviceIdType.MESH).start()

    def left(ref, sem):
        pltpu.make_async_remote_copy(
            src_ref=ref, dst_ref=ref, send_sem=sem, recv_sem=t_sems.at[0],
            device_id=to_core, device_id_type=pl.DeviceIdType.MESH).wait_send()

    def all_left(out):
        assert totals[out] % (8 * PW) == 0
        left(units_ref.at[pl.ds(0, totals[out] // (8 * PW))], out_sems.at[out])

    def arrive(dst, sem):
        pltpu.make_async_remote_copy(
            src_ref=dst, dst_ref=dst, send_sem=out_sems.at[0], recv_sem=sem,
            device_id=to_core, device_id_type=pl.DeviceIdType.MESH).wait_recv()

    OUT_T, OUT_W, OUT_MA, OUT_MB, OUT_D, OUT_K, OUT_KZ, OUT_KY, OUT_G, OUT_GS, OUT_GX, OUT_GC, OUT_KX = range(13)
    YD, XD, ZD = by_distance(NY), by_distance(NX), by_distance(NZ)

    sub = lax.broadcasted_iota(jnp.int32, (TR, WIDTH), 0) + row * TR
    lane = lax.broadcasted_iota(jnp.int32, (TR, WIDTH), 1)
    for a in range(NZ):
        tile = mat_ref[a]
        diag_part = jnp.where(sub > lane, tile, jnp.where(sub == lane, 0.5 * tile, 0.0))
        h_ref[a] = jnp.where(z < a, tile, jnp.where(z == a, diag_part, 0.0))

    tc_ref[x, y, core] = pan_ref[z]
    t_rows = pan_ref[...].reshape(NZ * TR, PW)
    gram = dot_tn(t_rows, t_rows)
    for l in range(NL):
        gl_ref[l] = gram[:, l * LW:(l + 1) * LW].reshape(NZ, 2, PW // NZ // 2, LW)
    XW = WIDTH // NX

    def columns(xb):
        return h_ref[:, :, pl.ds(pl.multiple_of(xb * XW, XW), XW)].reshape(NZ * TR, XW)

    for d in [0] + XD:
        xb = xp(d)
        terms = dot_split(columns(xb), t_rows, TN).reshape(NY, 2, TR, PW)
        for c in range(2):
            mpa_ref[c, xb] = terms[:, c, :, :LA]
            mpb_ref[c, :, xb] = terms[:, c, :, LA:]
    pl.semaphore_wait(barrier, len(peers))

    own_t = pan_ref.at[z]
    for d in YD:
        send(own_t, tc_ref.at[x, y, core], t_sems.at[d], to_y(d), OUT_T)
    for d in XD:
        send(own_t, tc_ref.at[x, y, core], t_sems.at[NY + d], to_x(d), OUT_T)
    send(gl_ref.at[:, z, other], gc_ref, g_sems.at[0], to_core, OUT_G)
    send(mpb_ref.at[other], cb_ref, mb_sems.at[0], to_core, OUT_MB)
    send(mpa_ref.at[other], ca_ref, ma_sems.at[0], to_core, OUT_MA)

    holds_g = x < NL
    own_l = lax.min(x, NL - 1)
    arrive(gc_ref, g_sems.at[0])
    gsum_ref[...] = gl_ref[:, z, core] + gc_ref[...]
    for d in XD:
        @pl.when(xp(d) < NL)
        def _():
            pltpu.make_async_remote_copy(
                src_ref=gsum_ref.at[lax.min(xp(d), NL - 1)], dst_ref=gx_ref.at[d - 1],
                send_sem=ky_out_sems.at[NY + d], recv_sem=g_sems.at[d],
                device_id=to_x(d), device_id_type=pl.DeviceIdType.MESH).start()

    def forward_t(ds):
        for d in ds:
            tile = tc_ref.at[x, yp(NY - d), core]
            arrive(tile, t_sems.at[d])
            for dx in XD:
                send(tile, tile, t_sems.at[NY + dx], to_x(dx), OUT_T)

    forward_t(YD[:3])

    @pl.when(holds_g)
    def _():
        gs = gsum_ref[own_l]
        for d in XD:
            arrive(gx_ref.at[d - 1], g_sems.at[d])
            gs = gs + gx_ref[d - 1]
        gsx_ref[...] = gs
        for d in YD:
            send(gsx_ref, gy_ref.at[d - 1], g_sems.at[NX + d], to_y(d), OUT_GS)

    arrive(cb_ref, mb_sems.at[0])
    mpb_ref[core] = mpb_ref[core] + cb_ref[...]
    for d in YD:
        send(mpb_ref.at[core, yp(d)], by_ref.at[d - 1], mb_sems.at[d], to_y(d), OUT_MB)

    forward_t(YD[3:])
    send(tc_ref.at[x, :, core], tc_ref.at[x, :, core], t_sems.at[NY + NX], to_core, OUT_T)
    arrive(ca_ref, ma_sems.at[0])
    mpa_ref[core] = mpa_ref[core] + ca_ref[...]

    def project(xb):
        tiles = tc_ref[xb, :, core].reshape(NY * TR, PW)
        return (dot_split(tiles, mpa_ref[core, xb].reshape(NY * TR, LA), TN),
                dot_split(tiles, mpb_ref[core, :, xb].reshape(NY * TR, PW - LA), TN))

    ka, kb = project(x)
    for dx in XD:
        xb = xp(NX - dx)
        arrive(tc_ref.at[xb, :, core], t_sems.at[NY + dx])
        send(tc_ref.at[xb, :, core], tc_ref.at[xb, :, core], t_sems.at[NY + NX + dx], to_core, OUT_T)
        more_a, more_b = project(xb)
        ka, kb = ka + more_a, kb + more_b
        if dx == XD[min(1, len(XD) - 1)]:
            @pl.when(holds_g)
            def _():
                gs = gsx_ref[...]
                for d in YD:
                    arrive(gy_ref.at[d - 1], g_sems.at[NX + d])
                    gs = gs + gy_ref[d - 1]
                g_ref[own_l, z, core] = gs
                own_g = g_ref.at[own_l, z, core]
                for d in ZD:
                    send(own_g, own_g, gz_sems.at[d - 1], to_z(d), OUT_GS)
    terms = jnp.concatenate([ka, kb], axis=1)
    block = lambda i, j: terms[i * LW:(i + 1) * LW, j * LW:(j + 1) * LW]
    lower = [block(i, j) + block(j, i).T for i, j in PAIRS]
    kp_ref[...] = jnp.concatenate(lower, axis=0).reshape(2, NX, NP, KR, LW)
    send(kp_ref.at[other], kc_ref, k_sems.at[0], to_core, OUT_K)

    arrive(tc_ref.at[x, :, other], t_sems.at[NY + NX])
    direct = dot_split(columns(x), tc_ref[x].reshape(XW, PW), NN)

    arrive(kc_ref, k_sems.at[0])
    ks_ref[...] = kp_ref[core] + kc_ref[...]
    for d in XD:
        send(ks_ref.at[xp(d)], kx_ref.at[d - 1], k_sems.at[d], to_x(d), OUT_K)

    for dx in XD:
        xb = xp(NX - dx)
        arrive(tc_ref.at[xb, :, other], t_sems.at[NY + NX + dx])
        direct = direct + dot_split(columns(xb), tc_ref[xb].reshape(XW, PW), NN)
    dp_ref[...] = direct.reshape(NZ, TR, PW)
    for d in ZD:
        send(dp_ref.at[zp(d)], rz_ref.at[d - 1], dz_sems.at[d - 1], to_z(d), OUT_D)

    for d in XD:
        send(mpa_ref.at[core, xp(d)], ax_ref.at[d - 1], ma_sems.at[d], to_x(d), OUT_MA)

    ksum = ks_ref[x]
    for d in XD:
        arrive(kx_ref.at[d - 1], k_sems.at[d])
        ksum = ksum + kx_ref[d - 1]
    ks_ref[x] = ksum
    for d in YD:
        @pl.when(yp(d) < NP)
        def _():
            pltpu.make_async_remote_copy(
                src_ref=ks_ref.at[x, lax.min(yp(d), NP - 1)], dst_ref=ky_ref.at[d - 1],
                send_sem=ky_out_sems.at[d], recv_sem=k_sems.at[NX + d],
                device_id=to_y(d), device_id_type=pl.DeviceIdType.MESH).start()

    part = mpb_ref[core, y]
    for d in YD:
        arrive(by_ref.at[d - 1], mb_sems.at[d])
        part = part + by_ref[d - 1]
    bs_ref[...] = part
    for d in XD:
        send(bs_ref.at[xp(d)], bx_ref.at[d - 1], mb_sems.at[NY + d], to_x(d), OUT_MB)

    part = mpa_ref[core, x]
    for d in XD:
        arrive(ax_ref.at[d - 1], ma_sems.at[d])
        part = part + ax_ref[d - 1]
    mpa_ref[core, x] = part
    for d in YD:
        send(mpa_ref.at[core, x, yp(d)], ay_ref.at[d - 1], ma_sems.at[NX + d], to_y(d), OUT_MA)

    own_g = g_ref.at[own_l, :, core]

    @pl.when(holds_g)
    def _():
        for d in ZD:
            arrive(g_ref.at[own_l, zp(NZ - d), core], gz_sems.at[d - 1])
        for d in XD:
            send(own_g, own_g, ga_sems.at[d], to_x(d), OUT_GX)

    held = y < NP
    yy = lax.min(y, NP - 1)

    @pl.when(held)
    def _():
        ksum = ks_ref[x, yy]
        for d in YD:
            arrive(ky_ref.at[d - 1], k_sems.at[NX + d])
            ksum = ksum + ky_ref[d - 1]
        kf_ref[...] = ksum
        for d in ZD:
            send(kf_ref, kz_ref.at[d - 1], kz_sems.at[d - 1], to_z(d), OUT_KZ)

    part_b = bs_ref[x]
    for d in XD:
        arrive(bx_ref.at[d - 1], mb_sems.at[NY + d])
        part_b = part_b + bx_ref[d - 1]
    part_a = mpa_ref[core, x, y]
    for d in YD:
        arrive(ay_ref.at[d - 1], ma_sems.at[NX + d])
        part_a = part_a + ay_ref[d - 1]
    wsum = dp_ref[z]
    for d in ZD:
        arrive(rz_ref.at[d - 1], dz_sems.at[d - 1])
        wsum = wsum + rz_ref[d - 1]
    wr_ref[z, :, :LA] = wsum[:, :LA] + part_a
    wr_ref[z, :, LA:] = wsum[:, LA:] + part_b
    wc_ref[x, y, core] = wr_ref[z]
    own_w = wc_ref.at[x, y, core]
    for d in YD:
        send(own_w, own_w, w_sems.at[d], to_y(d), OUT_W)
    for d in XD:
        send(own_w, own_w, w_sems.at[NY + d], to_x(d), OUT_W)
    for d in ZD:
        send(wr_ref.at[z], wr_ref.at[z], wz_sems.at[d - 1], to_z(d), OUT_W)

    for d in XD:
        src_l = xp(NX - d)

        @pl.when(src_l < NL)
        def _():
            arrive(g_ref.at[lax.min(src_l, NL - 1), :, core], ga_sems.at[d])
    send(g_ref.at[:, :, core], g_ref.at[:, :, core], ga_sems.at[0], to_core, OUT_GC)

    own_k = k_ref.at[core, x, yy]

    @pl.when(held)
    def _():
        ksum = kf_ref[...]
        for d in ZD:
            arrive(kz_ref.at[d - 1], kz_sems.at[d - 1])
            ksum = ksum + kz_ref[d - 1]
        k_ref[core, x, yy] = ksum
        for d in YD:
            send(own_k, own_k, ka_sems.at[d], to_y(d), OUT_KY)
        for d in XD:
            send(own_k, own_k, ka_sems.at[NY + d], to_x(d), OUT_KX)

    arrive(g_ref.at[:, :, other], ga_sems.at[0])
    whole = jnp.concatenate([g_ref[l].reshape(PW, LW) for l in range(NL)], axis=1)
    scaled, eye, s_row, s_col, start = scaled_gram(whole)
    sg_ref[...] = scaled
    inv_ref[...] = start

    def newton(dot):
        residual = eye - dot(sg_ref[...], inv_ref[...])
        inv_ref[...] += dot(inv_ref[...], residual)

    coarse = lambda a, b: jnp.dot(a.astype(jnp.bfloat16), b.astype(jnp.bfloat16),
                                  preferred_element_type=jnp.float32)
    fine = lambda a, b: dot_split(a, b, NN)

    for n, d in enumerate(YD):
        tile = wc_ref.at[x, yp(NY - d), core]
        arrive(tile, w_sems.at[d])
        for dx in XD:
            send(tile, tile, w_sems.at[NY + dx], to_x(dx), OUT_W)
        if n < COARSE_STEPS:
            newton(coarse)
    send(wc_ref.at[x, :, core], wc_ref.at[x, :, core], w_sems.at[NY + NX], to_core, OUT_W)
    for _ in range(COARSE_STEPS - len(YD)):
        newton(coarse)

    def forward_k(ds):
        for d in ds:
            src_y = yp(NY - d)

            @pl.when(src_y < NP)
            def _():
                piece = k_ref.at[core, x, lax.min(src_y, NP - 1)]
                arrive(piece, ka_sems.at[d])
                for dx in XD:
                    send(piece, piece, ka_sems.at[NY + dx], to_x(dx), OUT_KX)

    def pass_w(dx):
        block = wc_ref.at[xp(NX - dx), :, core]
        arrive(block, w_sems.at[NY + dx])
        send(block, block, w_sems.at[NY + NX + dx], to_core, OUT_W)

    def pass_k(dx):
        block = k_ref.at[core, xp(NX - dx)]
        if dx:
            arrive(block, ka_sems.at[NY + dx])
        send(block, block, ka_sems.at[NY + NX + dx], to_core, OUT_K)

    forward_k(YD[:3])
    newton(fine)
    forward_k(YD[3:])
    pass_k(0)
    residual = eye - dot_nn(sg_ref[...], inv_ref[...])
    err_ref[...] = jnp.full(err_ref.shape, jnp.sum(residual * residual), jnp.float32)
    inv_ref[...] = (inv_ref[...] + fine(inv_ref[...], residual)) * s_row * s_col
    for dx in XD:
        pass_w(dx)
    for dx in XD:
        pass_k(dx)
    left_ref[...] = dot_nn(pan_ref[...].reshape(NZ * TR, PW), inv_ref[...])

    for d in ZD:
        arrive(wr_ref.at[zp(NZ - d)], wz_sems.at[d - 1])
    arrive(wc_ref.at[x, :, other], w_sems.at[NY + NX])
    for dx in XD:
        arrive(wc_ref.at[xp(NX - dx), :, other], w_sems.at[NY + NX + dx])
    for dx in [0] + XD:
        arrive(k_ref.at[other, xp(NX - dx)], ka_sems.at[NY + NX + dx])
    for out in (OUT_T, OUT_W, OUT_MA, OUT_MB, OUT_D, OUT_K):
        all_left(out)
    left(g_ref.at[:, :, core], out_sems.at[OUT_GC])
    left(kx_ref, out_sems.at[OUT_KX])
    left(gc_ref, out_sems.at[OUT_G])
    for d in XD:
        pl.when(xp(d) < NL)(functools.partial(left, gx_ref.at[d - 1], ky_out_sems.at[NY + d]))
    for d in YD:
        pl.when(yp(d) < NP)(functools.partial(left, ky_ref.at[d - 1], ky_out_sems.at[d]))

    @pl.when(held)
    def _():
        left(kz_ref, out_sems.at[OUT_KZ])
        left(ky_ref, out_sems.at[OUT_KY])

    @pl.when(holds_g)
    def _():
        all_left(OUT_GS)
        all_left(OUT_GX)


def exchange(matrix, panel, sizes):
    NX, NY, NZ, TR, WIDTH, PW, NL, LA = sizes
    f32 = jnp.float32
    GR = PW // NZ // 2
    LW, LB = PW // NL, PW - LA
    NP = NL * (NL + 1) // 2 * LW // 2 // NX // KR
    vmem = pl.BlockSpec(memory_space=pltpu.VMEM)
    shape = lambda *s: jax.ShapeDtypeStruct(s, f32)
    V = lambda *s: pltpu.VMEM(s, f32)
    D = lambda n: pltpu.SemaphoreType.DMA((n,))
    return pl.pallas_call(
        functools.partial(comm_kernel, sizes),
        out_shape=[shape(NL, NZ, 2, GR, LW), shape(2, NX, NP, KR, LW), shape(NX, NY, 2, TR, PW),
                   shape(NX, NY, 2, TR, PW), shape(NZ, TR, PW), shape(PW, PW), shape(8, 128),
                   shape(NZ * TR, PW)],
        in_specs=[vmem] * 2,
        out_specs=[vmem] * 8,
        scratch_shapes=[
            V(PW, PW), V(160, 8, PW), V(NZ, TR, WIDTH),
            V(NL, NZ, 2, GR, LW), V(NL, GR, LW), V(NL, GR, LW), V(NX - 1, GR, LW), V(GR, LW),
            V(NY - 1, GR, LW),
            V(2, NX, NY, TR, LA), V(2, NY, NX, TR, LB), V(NX, NY, TR, LA), V(NY, NX, TR, LB),
            V(NX - 1, NY, TR, LA), V(NY - 1, TR, LA), V(NY - 1, NX, TR, LB), V(NX, TR, LB),
            V(NX - 1, TR, LB),
            V(NZ, TR, PW), V(NZ - 1, TR, PW), V(2, NX, NP, KR, LW), V(NX, NP, KR, LW),
            V(NX - 1, NP, KR, LW), V(NX, NP, KR, LW), V(NY - 1, KR, LW), V(NZ - 1, KR, LW), V(KR, LW),
            D(13), D(NY + NX), D(NY + 2 * NX), D(NY + 2 * NX), D(NZ - 1), D(NX + NY), D(NX + NY),
            D(NZ - 1), D(NX + NY), D(NZ - 1), D(NX), D(NX + NY), D(NZ - 1), D(2 * NX + NY),
        ],
        compiler_params=pltpu.CompilerParams(
            collective_id=0, has_side_effects=True, vmem_limit_bytes=32 * 2**20),
        name="exchange",
    )(matrix, panel)


def polish(g_ref, n_ref, error):
    blocks, _, _, _, width = g_ref.shape
    size = blocks * width
    gram = jnp.concatenate([g_ref[l].reshape(size, width) for l in range(blocks)], axis=1)
    scaled, eye, s_row, s_col, start = scaled_gram(gram)
    usable = error < 0.25
    guess = n_ref[...] / s_row / s_col

    def step(state):
        count, _, guess = state
        residual = eye - dot_nn(scaled, guess)
        error = jnp.sum(residual * residual)
        return count + 1, error, guess + dot_nn(guess, residual)

    def again(state):
        return jnp.logical_and(state[1] > SMALL, state[0] < 80)

    state = (0, jnp.where(usable, error, 1.0), jnp.where(usable, guess, start))
    _, _, found = lax.while_loop(again, step, state)
    n_ref[...] = found * s_row * s_col


def finish_kernel(mat_ref, pan_ref, g_ref, k_ref, tc_ref, wc_ref, wr_ref, inv_ref, err_ref, left_ref,
                  out_ref, n_ref, tn_ref):
    NZ, TR, WIDTH = mat_ref.shape
    PW = pan_ref.shape[2]
    row = lax.axis_index("row")
    z = lax.axis_index("col")
    n_ref[...] = inv_ref[...]
    tn_ref[...] = left_ref[...]
    error = err_ref[0, 0]
    t_rows = pan_ref[...].reshape(NZ * TR, PW)

    @pl.when(jnp.logical_not(error <= SMALL))
    def _():
        polish(g_ref, n_ref, error)
        tn_ref[...] = dot_nn(t_rows, n_ref[...])

    size = k_ref.shape[-1]
    count = PW // size
    lower = k_ref[...].reshape(-1, size)
    block = lambda i, j: lower[(i * (i + 1) // 2 + j) * size:(i * (i + 1) // 2 + j + 1) * size]
    proj = jnp.concatenate([
        jnp.concatenate([block(i, j) if i >= j else block(j, i).T for j in range(count)], axis=1)
        for i in range(count)], axis=0)
    left = tn_ref[...]
    w_rows = wr_ref[...].reshape(NZ * TR, PW)
    right = dot_split(w_rows - 2.0 * dot_split(left, proj, NN), n_ref[...], NN)
    sub = lax.broadcasted_iota(jnp.int32, (TR, WIDTH), 0) + row * TR
    lane = lax.broadcasted_iota(jnp.int32, (TR, WIDTH), 1)
    change = dot_split(left, wc_ref[...], NT) + dot_split(right, tc_ref[...], NT)
    change = change.reshape(NZ, TR, WIDTH)
    for a in range(NZ):
        new = mat_ref[a] - 2.0 * change[a]
        keep = jnp.logical_or(z < a, jnp.logical_and(z == a, sub >= lane))
        out_ref[a] = jnp.where(keep, new, 0.0)


def finish(*operands):
    matrix = operands[0]
    vmem = pl.BlockSpec(memory_space=pltpu.VMEM)
    return pl.pallas_call(
        finish_kernel,
        out_shape=jax.ShapeDtypeStruct(matrix.shape, jnp.float32),
        in_specs=[vmem] * len(operands),
        out_specs=vmem,
        scratch_shapes=[pltpu.VMEM(operands[7].shape, jnp.float32), pltpu.VMEM(operands[9].shape, jnp.float32)],
        compiler_params=pltpu.CompilerParams(vmem_limit_bytes=32 * 2**20),
        name="finish",
    )(*operands)


def per_device(matrix, panel):
    NZ, _, TR, WIDTH = matrix.shape
    PW = panel.shape[3]
    NX, NY = PLANES[lax.axis_size("row")]
    lanes = max(PW // 128, 1)
    sizes = (NX, NY, NZ, TR, WIDTH, PW, lanes, PW // lanes if lanes > 1 else PW // 2)
    mat = matrix.reshape(NZ, TR, WIDTH)
    pan = panel.reshape(NZ, TR, PW)
    gram, proj, t_cols, w_cols, w_rows, guess, error, left = exchange(mat, pan, sizes)
    out = finish(mat, pan, gram, proj,
                 t_cols.reshape(WIDTH, PW), w_cols.reshape(WIDTH, PW), w_rows, guess, error, left)
    return out.reshape(NZ, 1, TR, WIDTH)


def solution(mesh):
    in_specs = (P(None, "row", None, "col"), P(None, "row", None, None))
    out_specs = P(None, "row", None, "col")
    return jax.shard_map(
        per_device, mesh=mesh, in_specs=in_specs, out_specs=out_specs, check_vma=False)
```

```python
import functools

import jax
import jax.numpy as jnp
from jax import lax
from jax.experimental import pallas as pl
from jax.experimental.pallas import tpu as pltpu
from jax.sharding import PartitionSpec as P

EXACT = lax.Precision.HIGHEST
PLANES = {64: (4, 8), 8: (2, 2)}


def dot_nn(a, b):
    return lax.dot_general(a, b, (((1,), (0,)), ((), ())), precision=EXACT,
                           preferred_element_type=jnp.float32)


def dot_tn(a, b):
    return lax.dot_general(a, b, (((0,), (0,)), ((), ())), precision=EXACT,
                           preferred_element_type=jnp.float32)


def dot_nt(a, b):
    return lax.dot_general(a, b, (((1,), (1,)), ((), ())), precision=EXACT,
                           preferred_element_type=jnp.float32)


def two_parts(a):
    high = a.astype(jnp.bfloat16)
    return high, (a - high.astype(jnp.float32)).astype(jnp.bfloat16)


def dot_split(a, b, dims):
    ah, al = two_parts(a)
    bh, bl = two_parts(b)
    dot = lambda p, q: lax.dot_general(p, q, (dims, ((), ())), preferred_element_type=jnp.float32)
    return dot(ah, bh) + (dot(ah, bl) + dot(al, bh))


NN, TN, NT = ((1,), (0,)), ((0,), (0,)), ((1,), (1,))


def by_distance(n):
    return sorted(range(1, n), key=lambda d: (min(d, n - d), d))


def scaled_gram(gram):
    n = gram.shape[0]
    eye = jnp.where(lax.broadcasted_iota(jnp.int32, (n, n), 0)
                    == lax.broadcasted_iota(jnp.int32, (n, n), 1), 1.0, 0.0)
    diag = gram * eye
    s_row = lax.rsqrt(jnp.sum(diag, axis=0, keepdims=True))
    s_col = lax.rsqrt(jnp.sum(diag, axis=1, keepdims=True))
    scaled = gram * s_row * s_col
    bound = jnp.max(jnp.sum(jnp.abs(scaled), axis=0, keepdims=True))
    return scaled, eye, s_row, s_col, eye * (2.0 / (1.0 + bound))


COARSE_STEPS = 5
SMALL = 1e-6
KR = 16


def comm_kernel(sizes, mat_ref, pan_ref, g_ref, k_ref, tc_ref, wc_ref, wr_ref, inv_ref, err_ref, left_ref,
                sg_ref, units_ref, h_ref,
                gl_ref, gc_ref, gsum_ref, gx_ref, gsx_ref, gy_ref,
                mpa_ref, mpb_ref, ca_ref, cb_ref, ax_ref, ay_ref, by_ref, bs_ref, bx_ref,
                dp_ref, rz_ref, ds_ref, kp_ref, kc_ref, kx_ref, ks_ref, ky_ref, kz_ref, kf_ref,
                out_sems, ky_out_sems, dz_out_sems, t_sems, w_sems, wz_sems, ma_sems, mb_sems, dz_sems,
                g_sems, gz_sems, ga_sems, k_sems, kz_sems, ka_sems):
    NX, NY, NZ, TR, WIDTH, PW, NL, LA = sizes
    LW = PW // NL
    PAIRS = [(i, j) for i in range(NL) for j in range(i + 1)]
    NP = len(PAIRS) * LW // 2 // NX // KR
    row = lax.axis_index("row")
    z = lax.axis_index("col")
    core = lax.rem(row, 2)
    chip = lax.div(row, 2)
    y = lax.rem(chip, NY)
    x = lax.div(chip, NY)
    other = 1 - core

    def at(x_, y_, c_):
        return (x_ * NY + y_) * 2 + c_

    def xp(d):
        return lax.rem(x + d, NX)

    def yp(d):
        return lax.rem(y + d, NY)

    def zp(d):
        return lax.rem(z + d, NZ)

    to_x = lambda d: (at(xp(d), y, core), z)
    to_y = lambda d: (at(x, yp(d), core), z)
    to_z = lambda d: (row, zp(d))
    to_core = (at(x, y, other), z)

    barrier = pltpu.get_barrier_semaphore()
    peers = ([to_x(d) for d in range(1, NX)] + [to_y(d) for d in range(1, NY)]
             + [to_z(d) for d in range(1, NZ)] + [to_core])
    for peer in peers:
        pl.semaphore_signal(barrier, inc=1, device_id=peer, device_id_type=pl.DeviceIdType.MESH)

    totals = {}

    def send(src, dst, sem, peer, out):
        words = 1
        for n in src.shape:
            words *= n
        totals[out] = totals.get(out, 0) + words
        pltpu.make_async_remote_copy(
            src_ref=src, dst_ref=dst, send_sem=out_sems.at[out], recv_sem=sem,
            device_id=peer, device_id_type=pl.DeviceIdType.MESH).start()

    def left(ref, sem):
        pltpu.make_async_remote_copy(
            src_ref=ref, dst_ref=ref, send_sem=sem, recv_sem=t_sems.at[0],
            device_id=to_core, device_id_type=pl.DeviceIdType.MESH).wait_send()

    def all_left(out):
        assert totals[out] % (8 * PW) == 0
        left(units_ref.at[pl.ds(0, totals[out] // (8 * PW))], out_sems.at[out])

    def arrive(dst, sem):
        pltpu.make_async_remote_copy(
            src_ref=dst, dst_ref=dst, send_sem=out_sems.at[0], recv_sem=sem,
            device_id=to_core, device_id_type=pl.DeviceIdType.MESH).wait_recv()

    OUT_T, OUT_W, OUT_MA, OUT_MB, OUT_D, OUT_K, OUT_KZ, OUT_KY, OUT_G, OUT_GS, OUT_GX, OUT_GC, OUT_KX = range(13)
    YD, XD, ZD = by_distance(NY), by_distance(NX), by_distance(NZ)

    sub = lax.broadcasted_iota(jnp.int32, (TR, WIDTH), 0) + row * TR
    lane = lax.broadcasted_iota(jnp.int32, (TR, WIDTH), 1)
    for a in range(NZ):
        tile = mat_ref[a]
        diag_part = jnp.where(sub > lane, tile, jnp.where(sub == lane, 0.5 * tile, 0.0))
        h_ref[a] = jnp.where(z < a, tile, jnp.where(z == a, diag_part, 0.0))

    tc_ref[x, y, core] = pan_ref[z]
    t_rows = pan_ref[...].reshape(NZ * TR, PW)
    gram = dot_tn(t_rows, t_rows)
    for l in range(NL):
        gl_ref[l] = gram[:, l * LW:(l + 1) * LW].reshape(NZ, 2, PW // NZ // 2, LW)
    XW = WIDTH // NX

    def columns(xb):
        return h_ref[:, :, pl.ds(pl.multiple_of(xb * XW, XW), XW)].reshape(NZ * TR, XW)

    for d in [0] + XD:
        xb = xp(d)
        terms = dot_split(columns(xb), t_rows, TN).reshape(NY, 2, TR, PW)
        for c in range(2):
            mpa_ref[c, xb] = terms[:, c, :, :LA]
            mpb_ref[c, :, xb] = terms[:, c, :, LA:]
    pl.semaphore_wait(barrier, len(peers))

    own_t = pan_ref.at[z]
    for d in YD:
        send(own_t, tc_ref.at[x, y, core], t_sems.at[d], to_y(d), OUT_T)
    for d in XD:
        send(own_t, tc_ref.at[x, y, core], t_sems.at[NY + d], to_x(d), OUT_T)
    send(gl_ref.at[:, z, other], gc_ref, g_sems.at[0], to_core, OUT_G)
    send(mpb_ref.at[other], cb_ref, mb_sems.at[0], to_core, OUT_MB)
    send(mpa_ref.at[other], ca_ref, ma_sems.at[0], to_core, OUT_MA)

    holds_g = x < NL
    own_l = lax.min(x, NL - 1)
    arrive(gc_ref, g_sems.at[0])
    gsum_ref[...] = gl_ref[:, z, core] + gc_ref[...]
    for d in XD:
        @pl.when(xp(d) < NL)
        def _():
            pltpu.make_async_remote_copy(
                src_ref=gsum_ref.at[lax.min(xp(d), NL - 1)], dst_ref=gx_ref.at[d - 1],
                send_sem=ky_out_sems.at[NY + d], recv_sem=g_sems.at[d],
                device_id=to_x(d), device_id_type=pl.DeviceIdType.MESH).start()

    def forward_t(ds):
        for d in ds:
            tile = tc_ref.at[x, yp(NY - d), core]
            arrive(tile, t_sems.at[d])
            for dx in XD:
                send(tile, tile, t_sems.at[NY + dx], to_x(dx), OUT_T)

    forward_t(YD[:3])

    @pl.when(holds_g)
    def _():
        gs = gsum_ref[own_l]
        for d in XD:
            arrive(gx_ref.at[d - 1], g_sems.at[d])
            gs = gs + gx_ref[d - 1]
        gsx_ref[...] = gs
        for d in YD:
            send(gsx_ref, gy_ref.at[d - 1], g_sems.at[NX + d], to_y(d), OUT_GS)

    arrive(cb_ref, mb_sems.at[0])
    mpb_ref[core] = mpb_ref[core] + cb_ref[...]
    for d in YD:
        send(mpb_ref.at[core, yp(d)], by_ref.at[d - 1], mb_sems.at[d], to_y(d), OUT_MB)

    forward_t(YD[3:])
    send(tc_ref.at[x, :, core], tc_ref.at[x, :, core], t_sems.at[NY + NX], to_core, OUT_T)
    arrive(ca_ref, ma_sems.at[0])
    mpa_ref[core] = mpa_ref[core] + ca_ref[...]

    def project(xb):
        tiles = tc_ref[xb, :, core].reshape(NY * TR, PW)
        return (dot_split(tiles, mpa_ref[core, xb].reshape(NY * TR, LA), TN),
                dot_split(tiles, mpb_ref[core, :, xb].reshape(NY * TR, PW - LA), TN))

    ka, kb = project(x)
    for dx in XD:
        xb = xp(NX - dx)
        arrive(tc_ref.at[xb, :, core], t_sems.at[NY + dx])
        send(tc_ref.at[xb, :, core], tc_ref.at[xb, :, core], t_sems.at[NY + NX + dx], to_core, OUT_T)
        more_a, more_b = project(xb)
        ka, kb = ka + more_a, kb + more_b
        if dx == XD[min(1, len(XD) - 1)]:
            @pl.when(holds_g)
            def _():
                gs = gsx_ref[...]
                for d in YD:
                    arrive(gy_ref.at[d - 1], g_sems.at[NX + d])
                    gs = gs + gy_ref[d - 1]
                g_ref[own_l, z, core] = gs
                own_g = g_ref.at[own_l, z, core]
                for d in ZD:
                    send(own_g, own_g, gz_sems.at[d - 1], to_z(d), OUT_GS)
    terms = jnp.concatenate([ka, kb], axis=1)
    block = lambda i, j: terms[i * LW:(i + 1) * LW, j * LW:(j + 1) * LW]
    lower = [block(i, j) + block(j, i).T for i, j in PAIRS]
    kp_ref[...] = jnp.concatenate(lower, axis=0).reshape(2, NX, NP, KR, LW)
    send(kp_ref.at[other], kc_ref, k_sems.at[0], to_core, OUT_K)

    arrive(tc_ref.at[x, :, other], t_sems.at[NY + NX])
    direct = dot_split(columns(x), tc_ref[x].reshape(XW, PW), NN)

    arrive(kc_ref, k_sems.at[0])
    ks_ref[...] = kp_ref[core] + kc_ref[...]
    for d in XD:
        send(ks_ref.at[xp(d)], kx_ref.at[d - 1], k_sems.at[d], to_x(d), OUT_K)

    for d in XD:
        send(mpa_ref.at[core, xp(d)], ax_ref.at[d - 1], ma_sems.at[d], to_x(d), OUT_MA)

    for dx in XD:
        xb = xp(NX - dx)
        arrive(tc_ref.at[xb, :, other], t_sems.at[NY + NX + dx])
        direct = direct + dot_split(columns(xb), tc_ref[xb].reshape(XW, PW), NN)
    dp_ref[...] = direct.reshape(NZ, TR, PW)
    for d in ZD:
        @pl.when(zp(d) > z)
        def _():
            pltpu.make_async_remote_copy(
                src_ref=dp_ref.at[zp(d)], dst_ref=rz_ref.at[d - 1],
                send_sem=dz_out_sems.at[d - 1], recv_sem=dz_sems.at[d - 1],
                device_id=to_z(d), device_id_type=pl.DeviceIdType.MESH).start()

    ksum = ks_ref[x]
    for d in XD:
        arrive(kx_ref.at[d - 1], k_sems.at[d])
        ksum = ksum + kx_ref[d - 1]
    ks_ref[x] = ksum
    for d in YD:
        @pl.when(yp(d) < NP)
        def _():
            pltpu.make_async_remote_copy(
                src_ref=ks_ref.at[x, lax.min(yp(d), NP - 1)], dst_ref=ky_ref.at[d - 1],
                send_sem=ky_out_sems.at[d], recv_sem=k_sems.at[NX + d],
                device_id=to_y(d), device_id_type=pl.DeviceIdType.MESH).start()

    part = mpb_ref[core, y]
    for d in YD:
        arrive(by_ref.at[d - 1], mb_sems.at[d])
        part = part + by_ref[d - 1]
    bs_ref[...] = part
    for d in XD:
        send(bs_ref.at[xp(d)], bx_ref.at[d - 1], mb_sems.at[NY + d], to_x(d), OUT_MB)

    part = mpa_ref[core, x]
    for d in XD:
        arrive(ax_ref.at[d - 1], ma_sems.at[d])
        part = part + ax_ref[d - 1]
    mpa_ref[core, x] = part
    for d in YD:
        send(mpa_ref.at[core, x, yp(d)], ay_ref.at[d - 1], ma_sems.at[NX + d], to_y(d), OUT_MA)

    own_g = g_ref.at[own_l, :, core]

    @pl.when(holds_g)
    def _():
        for d in ZD:
            arrive(g_ref.at[own_l, zp(NZ - d), core], gz_sems.at[d - 1])
        for d in XD:
            send(own_g, own_g, ga_sems.at[d], to_x(d), OUT_GX)

    held = y < NP
    yy = lax.min(y, NP - 1)

    @pl.when(held)
    def _():
        ksum = ks_ref[x, yy]
        for d in YD:
            arrive(ky_ref.at[d - 1], k_sems.at[NX + d])
            ksum = ksum + ky_ref[d - 1]
        kf_ref[...] = ksum
        for d in ZD:
            send(kf_ref, kz_ref.at[d - 1], kz_sems.at[d - 1], to_z(d), OUT_KZ)

    part_b = bs_ref[x]
    for d in XD:
        arrive(bx_ref.at[d - 1], mb_sems.at[NY + d])
        part_b = part_b + bx_ref[d - 1]
    part_a = mpa_ref[core, x, y]
    for d in YD:
        arrive(ay_ref.at[d - 1], ma_sems.at[NX + d])
        part_a = part_a + ay_ref[d - 1]
    ds_ref[...] = dp_ref[z]
    for d in ZD:
        @pl.when(zp(NZ - d) < z)
        def _():
            arrive(rz_ref.at[d - 1], dz_sems.at[d - 1])
            ds_ref[...] += rz_ref[d - 1]
    wsum = ds_ref[...]
    wr_ref[z, :, :LA] = wsum[:, :LA] + part_a
    wr_ref[z, :, LA:] = wsum[:, LA:] + part_b
    wc_ref[x, y, core] = wr_ref[z]
    own_w = wc_ref.at[x, y, core]
    for d in YD:
        send(own_w, own_w, w_sems.at[d], to_y(d), OUT_W)
    for d in XD:
        send(own_w, own_w, w_sems.at[NY + d], to_x(d), OUT_W)
    for d in ZD:
        send(wr_ref.at[z], wr_ref.at[z], wz_sems.at[d - 1], to_z(d), OUT_W)

    for d in XD:
        src_l = xp(NX - d)

        @pl.when(src_l < NL)
        def _():
            arrive(g_ref.at[lax.min(src_l, NL - 1), :, core], ga_sems.at[d])
    send(g_ref.at[:, :, core], g_ref.at[:, :, core], ga_sems.at[0], to_core, OUT_GC)

    own_k = k_ref.at[core, x, yy]

    @pl.when(held)
    def _():
        ksum = kf_ref[...]
        for d in ZD:
            arrive(kz_ref.at[d - 1], kz_sems.at[d - 1])
            ksum = ksum + kz_ref[d - 1]
        k_ref[core, x, yy] = ksum
        for d in YD:
            send(own_k, own_k, ka_sems.at[d], to_y(d), OUT_KY)
        for d in XD:
            send(own_k, own_k, ka_sems.at[NY + d], to_x(d), OUT_KX)

    arrive(g_ref.at[:, :, other], ga_sems.at[0])
    whole = jnp.concatenate([g_ref[l].reshape(PW, LW) for l in range(NL)], axis=1)
    scaled, eye, s_row, s_col, start = scaled_gram(whole)
    sg_ref[...] = scaled
    inv_ref[...] = start

    def newton(dot):
        residual = eye - dot(sg_ref[...], inv_ref[...])
        inv_ref[...] += dot(inv_ref[...], residual)

    coarse = lambda a, b: jnp.dot(a.astype(jnp.bfloat16), b.astype(jnp.bfloat16),
                                  preferred_element_type=jnp.float32)
    fine = lambda a, b: dot_split(a, b, NN)

    for n, d in enumerate(YD):
        tile = wc_ref.at[x, yp(NY - d), core]
        arrive(tile, w_sems.at[d])
        for dx in XD:
            send(tile, tile, w_sems.at[NY + dx], to_x(dx), OUT_W)
        if n < COARSE_STEPS:
            newton(coarse)
    send(wc_ref.at[x, :, core], wc_ref.at[x, :, core], w_sems.at[NY + NX], to_core, OUT_W)
    for _ in range(COARSE_STEPS - len(YD)):
        newton(coarse)

    def forward_k(ds):
        for d in ds:
            src_y = yp(NY - d)

            @pl.when(src_y < NP)
            def _():
                piece = k_ref.at[core, x, lax.min(src_y, NP - 1)]
                arrive(piece, ka_sems.at[d])
                for dx in XD:
                    send(piece, piece, ka_sems.at[NY + dx], to_x(dx), OUT_KX)

    def pass_w(dx):
        block = wc_ref.at[xp(NX - dx), :, core]
        arrive(block, w_sems.at[NY + dx])
        send(block, block, w_sems.at[NY + NX + dx], to_core, OUT_W)

    def pass_k(dx):
        block = k_ref.at[core, xp(NX - dx)]
        if dx:
            arrive(block, ka_sems.at[NY + dx])
        send(block, block, ka_sems.at[NY + NX + dx], to_core, OUT_K)

    forward_k(YD[:3])
    newton(fine)
    forward_k(YD[3:])
    pass_k(0)
    residual = eye - dot_nn(sg_ref[...], inv_ref[...])
    err_ref[...] = jnp.full(err_ref.shape, jnp.sum(residual * residual), jnp.float32)
    inv_ref[...] = (inv_ref[...] + fine(inv_ref[...], residual)) * s_row * s_col
    for dx in XD:
        pass_w(dx)
    for dx in XD:
        pass_k(dx)
    left_ref[...] = dot_nn(pan_ref[...].reshape(NZ * TR, PW), inv_ref[...])

    for d in ZD:
        arrive(wr_ref.at[zp(NZ - d)], wz_sems.at[d - 1])
    arrive(wc_ref.at[x, :, other], w_sems.at[NY + NX])
    for dx in XD:
        arrive(wc_ref.at[xp(NX - dx), :, other], w_sems.at[NY + NX + dx])
    for dx in [0] + XD:
        arrive(k_ref.at[other, xp(NX - dx)], ka_sems.at[NY + NX + dx])
    for d in ZD:
        pl.when(zp(d) > z)(functools.partial(left, rz_ref.at[d - 1], dz_out_sems.at[d - 1]))
    for out in (OUT_T, OUT_W, OUT_MA, OUT_MB, OUT_K):
        all_left(out)
    left(g_ref.at[:, :, core], out_sems.at[OUT_GC])
    left(kx_ref, out_sems.at[OUT_KX])
    left(gc_ref, out_sems.at[OUT_G])
    for d in XD:
        pl.when(xp(d) < NL)(functools.partial(left, gx_ref.at[d - 1], ky_out_sems.at[NY + d]))
    for d in YD:
        pl.when(yp(d) < NP)(functools.partial(left, ky_ref.at[d - 1], ky_out_sems.at[d]))

    @pl.when(held)
    def _():
        left(kz_ref, out_sems.at[OUT_KZ])
        left(ky_ref, out_sems.at[OUT_KY])

    @pl.when(holds_g)
    def _():
        all_left(OUT_GS)
        all_left(OUT_GX)


def exchange(matrix, panel, sizes):
    NX, NY, NZ, TR, WIDTH, PW, NL, LA = sizes
    f32 = jnp.float32
    GR = PW // NZ // 2
    LW, LB = PW // NL, PW - LA
    NP = NL * (NL + 1) // 2 * LW // 2 // NX // KR
    vmem = pl.BlockSpec(memory_space=pltpu.VMEM)
    shape = lambda *s: jax.ShapeDtypeStruct(s, f32)
    V = lambda *s: pltpu.VMEM(s, f32)
    D = lambda n: pltpu.SemaphoreType.DMA((n,))
    return pl.pallas_call(
        functools.partial(comm_kernel, sizes),
        out_shape=[shape(NL, NZ, 2, GR, LW), shape(2, NX, NP, KR, LW), shape(NX, NY, 2, TR, PW),
                   shape(NX, NY, 2, TR, PW), shape(NZ, TR, PW), shape(PW, PW), shape(8, 128),
                   shape(NZ * TR, PW)],
        in_specs=[vmem] * 2,
        out_specs=[vmem] * 8,
        scratch_shapes=[
            V(PW, PW), V(160, 8, PW), V(NZ, TR, WIDTH),
            V(NL, NZ, 2, GR, LW), V(NL, GR, LW), V(NL, GR, LW), V(NX - 1, GR, LW), V(GR, LW),
            V(NY - 1, GR, LW),
            V(2, NX, NY, TR, LA), V(2, NY, NX, TR, LB), V(NX, NY, TR, LA), V(NY, NX, TR, LB),
            V(NX - 1, NY, TR, LA), V(NY - 1, TR, LA), V(NY - 1, NX, TR, LB), V(NX, TR, LB),
            V(NX - 1, TR, LB),
            V(NZ, TR, PW), V(NZ - 1, TR, PW), V(TR, PW), V(2, NX, NP, KR, LW), V(NX, NP, KR, LW),
            V(NX - 1, NP, KR, LW), V(NX, NP, KR, LW), V(NY - 1, KR, LW), V(NZ - 1, KR, LW), V(KR, LW),
            D(13), D(NY + NX), D(NZ - 1), D(NY + 2 * NX), D(NY + 2 * NX), D(NZ - 1), D(NX + NY), D(NX + NY),
            D(NZ - 1), D(NX + NY), D(NZ - 1), D(NX), D(NX + NY), D(NZ - 1), D(2 * NX + NY),
        ],
        compiler_params=pltpu.CompilerParams(
            collective_id=0, has_side_effects=True, vmem_limit_bytes=32 * 2**20),
        name="exchange",
    )(matrix, panel)


def polish(g_ref, n_ref, error):
    blocks, _, _, _, width = g_ref.shape
    size = blocks * width
    gram = jnp.concatenate([g_ref[l].reshape(size, width) for l in range(blocks)], axis=1)
    scaled, eye, s_row, s_col, start = scaled_gram(gram)
    usable = error < 0.25
    guess = n_ref[...] / s_row / s_col

    def step(state):
        count, _, guess = state
        residual = eye - dot_nn(scaled, guess)
        error = jnp.sum(residual * residual)
        return count + 1, error, guess + dot_nn(guess, residual)

    def again(state):
        return jnp.logical_and(state[1] > SMALL, state[0] < 80)

    state = (0, jnp.where(usable, error, 1.0), jnp.where(usable, guess, start))
    _, _, found = lax.while_loop(again, step, state)
    n_ref[...] = found * s_row * s_col


def finish_kernel(mat_ref, pan_ref, g_ref, k_ref, tc_ref, wc_ref, wr_ref, inv_ref, err_ref, left_ref,
                  out_ref, n_ref, tn_ref):
    NZ, TR, WIDTH = mat_ref.shape
    PW = pan_ref.shape[2]
    row = lax.axis_index("row")
    z = lax.axis_index("col")
    n_ref[...] = inv_ref[...]
    tn_ref[...] = left_ref[...]
    error = err_ref[0, 0]
    t_rows = pan_ref[...].reshape(NZ * TR, PW)

    @pl.when(jnp.logical_not(error <= SMALL))
    def _():
        polish(g_ref, n_ref, error)
        tn_ref[...] = dot_nn(t_rows, n_ref[...])

    size = k_ref.shape[-1]
    count = PW // size
    lower = k_ref[...].reshape(-1, size)
    block = lambda i, j: lower[(i * (i + 1) // 2 + j) * size:(i * (i + 1) // 2 + j + 1) * size]
    proj = jnp.concatenate([
        jnp.concatenate([block(i, j) if i >= j else block(j, i).T for j in range(count)], axis=1)
        for i in range(count)], axis=0)
    left = tn_ref[...]
    w_rows = wr_ref[...].reshape(NZ * TR, PW)
    right = dot_split(w_rows - 2.0 * dot_split(left, proj, NN), n_ref[...], NN)
    sub = lax.broadcasted_iota(jnp.int32, (TR, WIDTH), 0) + row * TR
    lane = lax.broadcasted_iota(jnp.int32, (TR, WIDTH), 1)
    change = dot_split(left, wc_ref[...], NT) + dot_split(right, tc_ref[...], NT)
    change = change.reshape(NZ, TR, WIDTH)
    for a in range(NZ):
        new = mat_ref[a] - 2.0 * change[a]
        keep = jnp.logical_or(z < a, jnp.logical_and(z == a, sub >= lane))
        out_ref[a] = jnp.where(keep, new, 0.0)


def finish(*operands):
    matrix = operands[0]
    vmem = pl.BlockSpec(memory_space=pltpu.VMEM)
    return pl.pallas_call(
        finish_kernel,
        out_shape=jax.ShapeDtypeStruct(matrix.shape, jnp.float32),
        in_specs=[vmem] * len(operands),
        out_specs=vmem,
        scratch_shapes=[pltpu.VMEM(operands[7].shape, jnp.float32), pltpu.VMEM(operands[9].shape, jnp.float32)],
        compiler_params=pltpu.CompilerParams(vmem_limit_bytes=32 * 2**20),
        name="finish",
    )(*operands)


def per_device(matrix, panel):
    NZ, _, TR, WIDTH = matrix.shape
    PW = panel.shape[3]
    NX, NY = PLANES[lax.axis_size("row")]
    lanes = max(PW // 128, 1)
    sizes = (NX, NY, NZ, TR, WIDTH, PW, lanes, PW // lanes if lanes > 1 else PW // 2)
    mat = matrix.reshape(NZ, TR, WIDTH)
    pan = panel.reshape(NZ, TR, PW)
    gram, proj, t_cols, w_cols, w_rows, guess, error, left = exchange(mat, pan, sizes)
    out = finish(mat, pan, gram, proj,
                 t_cols.reshape(WIDTH, PW), w_cols.reshape(WIDTH, PW), w_rows, guess, error, left)
    return out.reshape(NZ, 1, TR, WIDTH)


def solution(mesh):
    in_specs = (P(None, "row", None, "col"), P(None, "row", None, None))
    out_specs = P(None, "row", None, "col")
    return jax.shard_map(
        per_device, mesh=mesh, in_specs=in_specs, out_specs=out_specs, check_vma=False)
```
